32 devices in a mesh: lat: 8 (over z, y), lev: 4 (over x, core).
Axes of the slice: x: 2, y: 2, z: 4, core: 2. Of those that a mesh axis runs over, the one named last changes fastest.
Arguments:
- column_state: bfloat16 [4, 16, 128, 256], P(None, 'lat', 'lev'), may hold values from -6 to 6
- column_target: bfloat16 [4, 16, 128, 256], P(None, 'lat', 'lev'), may hold values from -6 to 6
- member_noise: float32 [2, 16, 128, 256], P(None, 'lat', 'lev'), may hold values from -40 to 40
- land_mask: int32 [16, 256], P('lat'), may hold values 0 or 1
- legendre_basis: float32 [16, 86], P('lat'), may hold values from -0.625 to 0.625
- mode_filter: float32 [86], replicated, may hold values from 0.2 to 2
- weight_in: float32 [384, 256], P('lat', 'lev'), may hold values from -0.3125 to 0.3125
- weight_out: float32 [256, 128], P('lev', 'lat'), may hold values from -0.375 to 0.375
- moment_in: float32 [384, 256], P('lat', 'lev'), may hold values from -0.00012207031 to 0.00012207031
- second_in: float32 [384, 256], P('lat', 'lev'), may hold values from 3.3115596e-10 to 1.3221055e-09
- moment_out: float32 [256, 128], P('lev', 'lat'), may hold values from -0.00024414062 to 0.00024414062
- second_out: float32 [256, 128], P('lev', 'lat'), may hold values from 1.0365769e-09 to 4.138425e-09
Outputs:
- loss_value: float32 [], replicated
- new_weight_in: float32 [384, 256], P('lat', 'lev')
- new_moment_in: float32 [384, 256], P('lat', 'lev')
- new_second_in: float32 [384, 256], P('lat', 'lev')
- new_weight_out: float32 [256, 128], P('lev', 'lat')
- new_moment_out: float32 [256, 128], P('lev', 'lat')
- new_second_out: float32 [256, 128], P('lev', 'lat')
The draws below stay inside these ranges and needn't reach their ends.
All inputs are finite; a program needn't handle non-finite values. No bound on the sum of `land_mask` on one device may be relied on, other than what follows from the above.
Results may differ from the reference program's by a relative error of at most 0.0046.
Values may be sent and summed in bfloat16 or wider, within the bound.
No kernel may reach another device: no remote copies, remote signals or barrier semaphores. Data moves between devices by JAX's collectives and lax.ppermute only.
A program may use at most 64 MiB of HBM per device.

```python
import math
import jax
import jax.numpy as jnp
from jax import lax

F = 128
H = 256
K = 86
NLON = 256
MEMBERS = 2
STEP = 7
ITEMS = 4
NLAT = 16


def draw_member_noise(key, part):
    key_rows, key_values = jax.random.split(key, 2)
    row_scale = 10.0 ** jax.random.uniform(key_rows, (MEMBERS, NLAT, 1, 1), jnp.float32)
    values = jax.random.truncated_normal(key_values, -4.0, 4.0, (MEMBERS, NLAT, F, NLON), jnp.float32)
    return values * row_scale


def set_ends(entries, key, low, top_value):
    index_at = [jax.random.randint(jax.random.fold_in(key, axis), (), 0, length) for axis, length in enumerate(entries.shape)]
    longest = entries.shape.index(max(entries.shape))
    neighbour = index_at[:longest] + [(index_at[longest] + 1) % entries.shape[longest]] + index_at[longest + 1:]
    return entries.at[tuple(index_at)].set(low).at[tuple(neighbour)].set(top_value)


def level_of(key, dims, shards, least, top_value):
    def one(dim, parts):
        heights = jax.random.uniform(jax.random.fold_in(jax.random.fold_in(key, 6), dim), (parts,), jnp.float32, least / len(shards), top_value / len(shards))
        return jnp.repeat(jnp.exp(heights), dims[dim] // parts).reshape((-1,) + (1,) * (len(dims) - dim - 1))

    gain = one(*shards[0])
    for cut in shards[1:]:
        gain = gain * one(*cut)
    return gain


def bell_draw(stream_key, shape, spread, most, cuts=(), kind=jnp.bfloat16):
    level = level_of(stream_key, shape, cuts, -0.22, 0.18) if cuts else 1.0
    entries = jax.random.normal(stream_key, shape, jnp.float32) * spread * level
    return jnp.minimum(jnp.maximum(entries, -most), most).astype(kind)


def setup_inputs(seed: int = 0) -> dict:
    arg_keys = jax.random.split(jax.random.key(seed), 13)
    column_state = bell_draw(arg_keys[0], (ITEMS, NLAT, F, NLON), 1.0, 6.0, ((1, 8), (2, 4)))
    column_target = bell_draw(arg_keys[1], (ITEMS, NLAT, F, NLON), 1.0, 6.0, ((1, 8), (2, 4)))
    member_noise = draw_member_noise(jax.random.fold_in(arg_keys[12], 71), 0)
    land_mask = set_ends((jax.random.randint(arg_keys[3], (NLAT, NLON), 0, 3) < 2).astype(jnp.int32), jax.random.fold_in(arg_keys[3], 1), 0, 1)
    legendre_basis = bell_draw(arg_keys[4], (NLAT, K), K ** -0.5, 0.625, ((0, 8),), jnp.float32)
    mode_filter = jnp.clip(jnp.exp(jax.random.uniform(arg_keys[5], (K,), jnp.float32, math.log(0.2), math.log(2.0))), 0.2, 2.0)
    weight_in = bell_draw(arg_keys[6], (3 * F, H), (3 * F) ** -0.5, 0.3125, ((0, 8), (1, 4)), jnp.float32)
    weight_out = bell_draw(arg_keys[7], (H, F), H ** -0.5, 0.375, ((0, 4), (1, 8)), jnp.float32)
    moment_in = bell_draw(arg_keys[8], (3 * F, H), (0.11 * 1.3 / (F * (ITEMS * NLAT * NLON) ** 0.5)), 0.00012207031, ((0, 8), (1, 4)), jnp.float32)
    second_in = jnp.clip(jnp.exp(math.log(1.3221055361611889e-09) - 1.3843914 * jax.random.uniform(arg_keys[9], (3 * F, H), jnp.float32) ** level_of(arg_keys[9], (3 * F, H), ((0, 8), (1, 4)), -0.2, 0.2)), 3.3115596376198653e-10, 1.3221055361611889e-09)
    moment_out = bell_draw(arg_keys[10], (H, F), (0.11 * 2.3 / (F * (ITEMS * NLAT * NLON) ** 0.5)), 0.00024414062, ((0, 4), (1, 8)), jnp.float32)
    second_out = jnp.clip(jnp.exp(math.log(4.138425158117798e-09) - 1.3843914 * jax.random.uniform(arg_keys[11], (H, F), jnp.float32) ** level_of(arg_keys[11], (H, F), ((0, 4), (1, 8)), -0.2, 0.2)), 1.036576935398159e-09, 4.138425158117798e-09)
    return dict(column_state=column_state, column_target=column_target, member_noise=member_noise, land_mask=land_mask, legendre_basis=legendre_basis, mode_filter=mode_filter, weight_in=weight_in, weight_out=weight_out, moment_in=moment_in, second_in=second_in, moment_out=moment_out, second_out=second_out)


@jax.custom_vjp
def low(v):
    return lax.optimization_barrier(v.astype(jnp.bfloat16)).astype(jnp.float32)

@jax.custom_vjp
def low_back(v):
    return v

def low_keep(v):
    return (low(v), None)

def low_pass(kept, grad):
    return (grad,)

def back_keep(v):
    return (v, None)

def back_low(kept, grad):
    return (low(grad),)
low.defvjp(low_keep, low_pass)
low_back.defvjp(back_keep, back_low)
HIGHEST_PRECISION = lax.Precision.HIGHEST
NOISE_SCALE = 0.5
LEARN_RATE = 0.02
BETA_ONE = 0.9
BETA_TWO = 0.95
EPSILON = 1e-08
WEIGHT_DECAY = 0.1

def latitude_weights(row_total):
    row_index = jnp.arange(row_total, dtype=jnp.float32)
    return jnp.cos((row_index + 0.5) * (math.pi / row_total) - 0.5 * math.pi)

def spectral(values_in, legendre_basis, mode_filter):
    rounded = low(legendre_basis)
    coefficients = jnp.einsum('nk,imnlf->imklf', rounded, values_in, precision=HIGHEST_PRECISION)
    filtered = low(mode_filter[None, None, :, None, None] * low_back(coefficients))
    return low_back(jnp.einsum('nk,imklf->imnlf', rounded, filtered, precision=HIGHEST_PRECISION))

def forward(weight_in, weight_out, inputs, state_full, target_full, legendre_basis, mode_filter, cell_weight, normaliser):
    row_total = inputs.shape[2]
    padded = jnp.pad(inputs, ((0, 0), (0, 0), (1, 1), (0, 0), (0, 0)))
    stacked = jnp.concatenate([padded[:, :, 0:row_total], padded[:, :, 1:row_total + 1], padded[:, :, 2:row_total + 2]], axis=-1)
    pre_act = low_back(jnp.einsum('imnlc,ch->imnlh', stacked, low(weight_in), precision=HIGHEST_PRECISION))
    hidden = low(jax.nn.silu(pre_act))
    branch = jnp.einsum('imnlh,hf->imnlf', hidden, low(weight_out), precision=HIGHEST_PRECISION)
    tendency = spectral(low(low_back(branch)), legendre_basis, mode_filter)
    prediction = state_full[:, None] + tendency
    d_one = prediction[:, 0] - target_full
    d_two = prediction[:, 1] - target_full
    error_cell = 0.375 * (d_one * d_one + d_two * d_two) + 0.25 * d_one * d_two
    return jnp.sum(cell_weight[None, :, :, None] * error_cell) / normaliser

def adamw(weight, moment_one, moment_two, gradient):
    moment_one = BETA_ONE * moment_one + (1.0 - BETA_ONE) * gradient
    moment_two = BETA_TWO * moment_two + (1.0 - BETA_TWO) * gradient * gradient
    fix_one = 1.0 - BETA_ONE ** STEP
    fix_two = 1.0 - BETA_TWO ** STEP
    update = moment_one / fix_one / (jnp.sqrt(moment_two / fix_two) + EPSILON)
    return (weight - LEARN_RATE * (update + WEIGHT_DECAY * weight), moment_one, moment_two)

def reference(column_state, column_target, member_noise, land_mask, legendre_basis, mode_filter, weight_in, weight_out, moment_in, second_in, moment_out, second_out):
    state_full = jnp.transpose(column_state.astype(jnp.float32), (0, 1, 3, 2))
    target_full = jnp.transpose(column_target.astype(jnp.float32), (0, 1, 3, 2))
    noise_cells = jnp.transpose(member_noise, (0, 1, 3, 2))
    power = lax.optimization_barrier(jnp.mean(noise_cells * noise_cells, axis=(1, 2), keepdims=True))
    scaled = noise_cells * lax.rsqrt(power + 1e-05)
    inputs = low(state_full[:, None] + NOISE_SCALE * scaled[None])
    cell_weight = latitude_weights(NLAT)[:, None] * land_mask.astype(jnp.float32)
    normaliser = jnp.float32(ITEMS * F) * jnp.sum(cell_weight)

    def loss_of(first_weight, second_weight):
        return forward(first_weight, second_weight, inputs, state_full, target_full, legendre_basis, mode_filter, cell_weight, normaliser)
    loss_value, pullback = jax.vjp(loss_of, weight_in, weight_out)
    grad_in, grad_out = pullback(jnp.ones_like(loss_value))
    new_weight_in, new_moment_in, new_second_in = adamw(weight_in, moment_in, second_in, grad_in)
    new_weight_out, new_moment_out, new_second_out = adamw(weight_out, moment_out, second_out, grad_out)
    return (loss_value, new_weight_in, new_moment_in, new_second_in, new_weight_out, new_moment_out, new_second_out)
```

```python
import math

import jax
import jax.numpy as jnp
from jax import lax
from jax.sharding import PartitionSpec as P

STEP = 7
NOISE_SCALE = 0.5
LEARN_RATE = 0.02
BETA_ONE = 0.9
BETA_TWO = 0.95
EPSILON = 1e-08
WEIGHT_DECAY = 0.1
EVERY = ("lat", "lev")
BF = jnp.bfloat16
F32 = jnp.float32


def adamw(weight, moment_one, moment_two, gradient):
    moment_one = BETA_ONE * moment_one + (1.0 - BETA_ONE) * gradient
    moment_two = BETA_TWO * moment_two + (1.0 - BETA_TWO) * gradient * gradient
    fix_one = 1.0 - BETA_ONE**STEP
    fix_two = 1.0 - BETA_TWO**STEP
    update = moment_one / fix_one / (jnp.sqrt(moment_two / fix_two) + EPSILON)
    return (weight - LEARN_RATE * (update + WEIGHT_DECAY * weight), moment_one, moment_two)


def parts_of(value, count):
    terms = []
    for _ in range(count):
        term = value.astype(BF)
        terms.append(term)
        value = value - lax.optimization_barrier(term).astype(F32)
    return terms


def exchange(pieces, devices):
    flat = jnp.concatenate([p.reshape(devices, -1) for p in pieces], axis=1)
    size = flat.shape[1]
    flat = jnp.pad(flat, ((0, 0), (0, -size % 1024)))
    flat = lax.all_to_all(flat.reshape(devices, -1, 128), EVERY, 0, 0, tiled=True).reshape(devices, -1)
    out, start = [], 0
    for p in pieces:
        count = math.prod(p.shape[1:])
        out.append(lax.slice_in_dim(flat, start, start + count, axis=1).reshape(p.shape))
        start += count
    return out


def body(
    column_state,
    column_target,
    member_noise,
    land_mask,
    legendre_basis,
    mode_filter,
    weight_in,
    weight_out,
    moment_in,
    second_in,
    moment_out,
    second_out,
):
    items, rows, feats, lons = column_state.shape
    members = member_noise.shape[0]
    lats, levs = lax.axis_size("lat"), lax.axis_size("lev")
    devices = lats * levs
    lat_total, all_feats, own = lats * rows, levs * feats, lons // devices
    modes = legendre_basis.shape[1]

    def cut(field):
        field = jnp.moveaxis(field.astype(BF), -1, 0)
        return field.reshape((devices, own) + field.shape[1:])

    def every(value):
        return jnp.broadcast_to(value[None], (devices,) + value.shape)

    def whole(field):
        field = field.reshape(lats, levs, own, -1, rows, feats)
        return field.transpose(3, 0, 4, 2, 1, 5).reshape(-1, lat_total, own, all_feats)

    squares = jnp.sum(member_noise * member_noise, axis=(1, 3))
    mask_count = jnp.sum(land_mask, axis=1).astype(F32)
    got = exchange(
        [
            cut(column_state),
            cut(column_target),
            cut(member_noise),
            cut(land_mask),
            *[every(s) for s in parts_of(squares, 3)],
            every(mask_count.astype(BF)),
            every(legendre_basis.astype(BF)),
            every(weight_in.astype(BF)),
            every(weight_out.astype(BF)),
        ],
        devices,
    )
    state = whole(got[0]).astype(F32)
    target = whole(got[1]).astype(F32)
    noise = whole(got[2]).astype(F32)
    mask = got[3].reshape(lats, levs, own, rows)[:, 0].transpose(0, 2, 1).reshape(lat_total, own).astype(F32)
    squares = sum(g.astype(F32) for g in got[4:7]).reshape(lats, levs, members, feats).sum(0)
    power = squares.transpose(1, 0, 2).reshape(members, all_feats) / (lat_total * lons)
    counts = got[7].reshape(lats, levs, rows)[:, 0].reshape(lat_total).astype(F32)
    basis = got[8].reshape(lats, levs, rows, modes)[:, 0].reshape(lat_total, modes)
    full_in = got[9].reshape(lats, levs, *weight_in.shape).transpose(0, 2, 1, 3).reshape(3 * all_feats, -1)
    full_out = got[10].reshape(lats, levs, *weight_out.shape).transpose(1, 2, 0, 3).reshape(-1, all_feats)

    cosine = jnp.cos((jnp.arange(lat_total, dtype=F32) + 0.5) * (math.pi / lat_total) - 0.5 * math.pi)
    cell_weight = cosine[:, None] * mask
    normaliser = items * all_feats * jnp.sum(cosine * counts)

    scaled = noise * lax.rsqrt(power + 1e-05)[:, None, None, :]
    inputs = (state[:, None] + NOISE_SCALE * scaled[None]).astype(BF)
    padded = jnp.pad(inputs, ((0, 0), (0, 0), (1, 1), (0, 0), (0, 0)))
    stacked = jnp.concatenate([padded[:, :, t : t + lat_total] for t in range(3)], axis=-1)

    def spectral(field):
        coefficients = jnp.einsum("nk,imnlf->imklf", basis, field, preferred_element_type=F32)
        filtered = (mode_filter[:, None, None] * coefficients).astype(BF)
        return jnp.einsum("nk,imklf->imnlf", basis, filtered, preferred_element_type=F32)

    pre_act = jnp.einsum("imnlc,ch->imnlh", stacked, full_in, preferred_element_type=F32)
    hidden = jax.nn.silu(pre_act).astype(BF)
    branch = jnp.einsum("imnlh,hf->imnlf", hidden, full_out, preferred_element_type=F32).astype(BF)
    prediction = state[:, None] + spectral(branch)
    d_one = prediction[:, 0] - target
    d_two = prediction[:, 1] - target
    error_cell = 0.375 * (d_one * d_one + d_two * d_two) + 0.25 * d_one * d_two
    loss_part = jnp.sum(cell_weight[None, :, :, None] * error_cell) / normaliser
    cell_scale = cell_weight[None, :, :, None] / normaliser
    g_one = cell_scale * (0.75 * d_one + 0.25 * d_two)
    g_two = cell_scale * (0.75 * d_two + 0.25 * d_one)
    g_pred = jnp.stack([g_one, g_two], axis=1).astype(BF)
    g_branch = spectral(g_pred).astype(BF)
    g_hidden = jnp.einsum("imnlf,hf->imnlh", g_branch, full_out, preferred_element_type=F32)
    sigmoid = jax.nn.sigmoid(pre_act)
    g_pre = (g_hidden * sigmoid * (1.0 + pre_act * (1.0 - sigmoid))).astype(BF)
    grad_in = jnp.einsum("imnlc,imnlh->ch", stacked, g_pre, preferred_element_type=F32)
    grad_out = jnp.einsum("imnlh,imnlf->hf", hidden, g_branch, preferred_element_type=F32)

    k_in, h_in = weight_in.shape
    h_out, f_out = weight_out.shape
    back = exchange(
        [
            grad_in.astype(BF).reshape(lats, k_in, levs, h_in).transpose(0, 2, 1, 3).reshape(devices, -1),
            grad_out.astype(BF).reshape(levs, h_out, lats, f_out).transpose(2, 0, 1, 3).reshape(devices, -1),
            *[every(t[None]) for t in parts_of(loss_part, 3)],
        ],
        devices,
    )
    grad_in = jnp.sum(back[0].astype(F32), axis=0).reshape(k_in, h_in)
    grad_out = jnp.sum(back[1].astype(F32), axis=0).reshape(h_out, f_out)
    loss_value = sum(jnp.sum(b.astype(F32)) for b in back[2:5])
    new_in = adamw(weight_in, moment_in, second_in, grad_in)
    new_out = adamw(weight_out, moment_out, second_out, grad_out)
    return (loss_value, *new_in, *new_out)


def solution(mesh):
    field = P(None, "lat", "lev", None)
    row, first, second = P("lat", None), P("lat", "lev"), P("lev", "lat")
    return jax.shard_map(
        body,
        mesh=mesh,
        in_specs=(field, field, field, row, row, P(), first, second, first, first, second, second),
        out_specs=(P(), first, first, first, second, second, second),
        check_vma=False,
    )
```

```python
import math

import jax
import jax.numpy as jnp
from jax import lax
from jax.experimental import pallas as pl
from jax.experimental.pallas import tpu as pltpu
from jax.sharding import PartitionSpec as P

STEP = 7
NOISE_SCALE = 0.5
LEARN_RATE = 0.02
BETA_ONE = 0.9
BETA_TWO = 0.95
EPSILON = 1e-08
WEIGHT_DECAY = 0.1
EVERY = ("lat", "lev")
BF = jnp.bfloat16
F32 = jnp.float32


def adamw(weight, moment_one, moment_two, gradient):
    moment_one = BETA_ONE * moment_one + (1.0 - BETA_ONE) * gradient
    moment_two = BETA_TWO * moment_two + (1.0 - BETA_TWO) * gradient * gradient
    fix_one = 1.0 - BETA_ONE**STEP
    fix_two = 1.0 - BETA_TWO**STEP
    update = moment_one / fix_one / (jnp.sqrt(moment_two / fix_two) + EPSILON)
    return (weight - LEARN_RATE * (update + WEIGHT_DECAY * weight), moment_one, moment_two)


def parts_of(value, count):
    terms = []
    for _ in range(count):
        term = value.astype(BF)
        terms.append(term)
        value = value - lax.optimization_barrier(term).astype(F32)
    return terms


def exchange(pieces, devices):
    flat = jnp.concatenate([p.reshape(devices, -1) for p in pieces], axis=1)
    size = flat.shape[1]
    flat = jnp.pad(flat, ((0, 0), (0, -size % 1024)))
    flat = lax.all_to_all(flat.reshape(devices, -1, 128), EVERY, 0, 0, tiled=True).reshape(devices, -1)
    out, start = [], 0
    for p in pieces:
        count = math.prod(p.shape[1:])
        out.append(lax.slice_in_dim(flat, start, start + count, axis=1).reshape(p.shape))
        start += count
    return out


def plain_body(
    column_state,
    column_target,
    member_noise,
    land_mask,
    legendre_basis,
    mode_filter,
    weight_in,
    weight_out,
    moment_in,
    second_in,
    moment_out,
    second_out,
):
    items, rows, feats, lons = column_state.shape
    members = member_noise.shape[0]
    lats, levs = lax.axis_size("lat"), lax.axis_size("lev")
    devices = lats * levs
    lat_total, all_feats, own = lats * rows, levs * feats, lons // devices
    modes = legendre_basis.shape[1]

    def cut(field):
        field = jnp.moveaxis(field.astype(BF), -1, 0)
        return field.reshape((devices, own) + field.shape[1:])

    def every(value):
        return jnp.broadcast_to(value[None], (devices,) + value.shape)

    def whole(field):
        field = field.reshape(lats, levs, own, -1, rows, feats)
        return field.transpose(3, 0, 4, 2, 1, 5).reshape(-1, lat_total, own, all_feats)

    squares = jnp.sum(member_noise * member_noise, axis=(1, 3))
    mask_count = jnp.sum(land_mask, axis=1).astype(F32)
    got = exchange(
        [
            cut(column_state),
            cut(column_target),
            cut(member_noise),
            cut(land_mask),
            *[every(s) for s in parts_of(squares, 3)],
            every(mask_count.astype(BF)),
            every(legendre_basis.astype(BF)),
            every(weight_in.astype(BF)),
            every(weight_out.astype(BF)),
        ],
        devices,
    )
    state = whole(got[0]).astype(F32)
    target = whole(got[1]).astype(F32)
    noise = whole(got[2]).astype(F32)
    mask = got[3].reshape(lats, levs, own, rows)[:, 0].transpose(0, 2, 1).reshape(lat_total, own).astype(F32)
    squares = sum(g.astype(F32) for g in got[4:7]).reshape(lats, levs, members, feats).sum(0)
    power = squares.transpose(1, 0, 2).reshape(members, all_feats) / (lat_total * lons)
    counts = got[7].reshape(lats, levs, rows)[:, 0].reshape(lat_total).astype(F32)
    basis = got[8].reshape(lats, levs, rows, modes)[:, 0].reshape(lat_total, modes)
    full_in = got[9].reshape(lats, levs, *weight_in.shape).transpose(0, 2, 1, 3).reshape(3 * all_feats, -1)
    full_out = got[10].reshape(lats, levs, *weight_out.shape).transpose(1, 2, 0, 3).reshape(-1, all_feats)

    cosine = jnp.cos((jnp.arange(lat_total, dtype=F32) + 0.5) * (math.pi / lat_total) - 0.5 * math.pi)
    cell_weight = cosine[:, None] * mask
    normaliser = items * all_feats * jnp.sum(cosine * counts)

    scaled = noise * lax.rsqrt(power + 1e-05)[:, None, None, :]
    inputs = (state[:, None] + NOISE_SCALE * scaled[None]).astype(BF)
    padded = jnp.pad(inputs, ((0, 0), (0, 0), (1, 1), (0, 0), (0, 0)))
    stacked = jnp.concatenate([padded[:, :, t : t + lat_total] for t in range(3)], axis=-1)

    def spectral(field):
        coefficients = jnp.einsum("nk,imnlf->imklf", basis, field, preferred_element_type=F32)
        filtered = (mode_filter[:, None, None] * coefficients).astype(BF)
        return jnp.einsum("nk,imklf->imnlf", basis, filtered, preferred_element_type=F32)

    pre_act = jnp.einsum("imnlc,ch->imnlh", stacked, full_in, preferred_element_type=F32)
    hidden = jax.nn.silu(pre_act).astype(BF)
    branch = jnp.einsum("imnlh,hf->imnlf", hidden, full_out, preferred_element_type=F32).astype(BF)
    prediction = state[:, None] + spectral(branch)
    d_one = prediction[:, 0] - target
    d_two = prediction[:, 1] - target
    error_cell = 0.375 * (d_one * d_one + d_two * d_two) + 0.25 * d_one * d_two
    loss_part = jnp.sum(cell_weight[None, :, :, None] * error_cell) / normaliser
    cell_scale = cell_weight[None, :, :, None] / normaliser
    g_one = cell_scale * (0.75 * d_one + 0.25 * d_two)
    g_two = cell_scale * (0.75 * d_two + 0.25 * d_one)
    g_pred = jnp.stack([g_one, g_two], axis=1).astype(BF)
    g_branch = spectral(g_pred).astype(BF)
    g_hidden = jnp.einsum("imnlf,hf->imnlh", g_branch, full_out, preferred_element_type=F32)
    sigmoid = jax.nn.sigmoid(pre_act)
    g_pre = (g_hidden * sigmoid * (1.0 + pre_act * (1.0 - sigmoid))).astype(BF)
    grad_in = jnp.einsum("imnlc,imnlh->ch", stacked, g_pre, preferred_element_type=F32)
    grad_out = jnp.einsum("imnlh,imnlf->hf", hidden, g_branch, preferred_element_type=F32)

    k_in, h_in = weight_in.shape
    h_out, f_out = weight_out.shape
    back = exchange(
        [
            grad_in.astype(BF).reshape(lats, k_in, levs, h_in).transpose(0, 2, 1, 3).reshape(devices, -1),
            grad_out.astype(BF).reshape(levs, h_out, lats, f_out).transpose(2, 0, 1, 3).reshape(devices, -1),
            *[every(t[None]) for t in parts_of(loss_part, 3)],
        ],
        devices,
    )
    grad_in = jnp.sum(back[0].astype(F32), axis=0).reshape(k_in, h_in)
    grad_out = jnp.sum(back[1].astype(F32), axis=0).reshape(h_out, f_out)
    loss_value = sum(jnp.sum(b.astype(F32)) for b in back[2:5])
    new_in = adamw(weight_in, moment_in, second_in, grad_in)
    new_out = adamw(weight_out, moment_out, second_out, grad_out)
    return (loss_value, *new_in, *new_out)


LANES = 128
SUBLANES = 8
NT = (((1,), (1,)), ((), ()))
TN = (((0,), (0,)), ((), ()))
HIGHEST = lax.Precision.HIGHEST


def kernels_fit(arrays, lats, levs):
    items, rows, feats, lons = arrays[0].shape
    members, modes = arrays[2].shape[0], arrays[4].shape[1]
    devices = lats * levs
    return (
        lons == devices * SUBLANES
        and lats * rows * SUBLANES == LANES
        and (rows, feats, levs, members) == (2, LANES // 4, 4, 2)
        and items % 2 == 0
        and lons % LANES == 0
        and modes < LANES
        and arrays[6].shape[0] % 16 == 0
        and arrays[7].shape[1] % 16 == 0
        and arrays[6].shape[1] == arrays[7].shape[0] == LANES // 2
    )


def lane_index(shape):
    return lax.broadcasted_iota(jnp.int32, shape, len(shape) - 1)


def row_index(shape):
    return lax.broadcasted_iota(jnp.int32, shape, len(shape) - 2)


def halves(top, bottom):
    first = lane_index(top.shape) < LANES // 2
    turned_top, turned_bottom = pltpu.roll(top, LANES // 2, 1), pltpu.roll(bottom, LANES // 2, 1)
    return jnp.where(first, top, turned_bottom), jnp.where(first, turned_top, bottom)


def quarters(v):
    a0, a2 = halves(v[0], v[2])
    a1, a3 = halves(v[1], v[3])
    even = lane_index(a0.shape) // 32 % 2 == 0

    def pair(a, b):
        return jnp.where(even, a, pltpu.roll(b, 32, 1)), jnp.where(even, pltpu.roll(a, 96, 1), b)

    return (*pair(a0, a1), *pair(a2, a3))


def pack_kernel(state, target, noise, mask, basis, first, second, send, aux):
    devices, lons = send.shape[0], state.shape[1]
    eye = (row_index((lons, lons)) == lane_index((lons, lons))).astype(BF)

    def turned(rows):
        out = lax.dot_general(eye, rows.astype(BF), NT, preferred_element_type=F32)
        return [out[:, g : g + LANES].reshape(devices, SUBLANES, LANES) for g in range(0, out.shape[1], LANES)]

    fields = noise[...]
    groups = turned(state[...]) + turned(target[...]) + turned(fields)
    start = SUBLANES * len(groups)
    send[:, :start, :] = jnp.concatenate(groups, axis=1).astype(BF)

    def folded(rows):
        half = rows.shape[0] // 2
        return jnp.concatenate([rows[:half], rows[half:]], axis=1)

    weights = jnp.concatenate([folded(first[...]), folded(second[...])], axis=0).astype(BF)
    send[:, start : start + weights.shape[0], :] = jnp.broadcast_to(weights[None], (devices,) + weights.shape)
    start += weights.shape[0]

    squares = lax.dot_general(jnp.ones((SUBLANES, lons), F32), fields * fields, NT, precision=HIGHEST)
    count = squares.shape[1]
    source, feature = row_index((count, LANES)), lane_index((count, LANES)) % 32
    sums = []
    for member in range(2):
        pick = ((source // 64 == member) & (source % 32 == feature)).astype(F32)
        total = jnp.dot(squares, pick, precision=HIGHEST)
        high = total.astype(BF).astype(F32)
        sums += [high[:1], (total - high)[:1]]
    cells = mask[...].astype(F32)
    aux[...] = jnp.zeros_like(aux)
    aux[0:2, 0 : basis.shape[1]] = basis[...]
    counts = jnp.sum(cells, axis=1, keepdims=True)
    top = aux[0:2, :]
    top = jnp.where(lane_index(top.shape) == LANES - 1, counts, top)
    share = LANES // SUBLANES
    for g in range(lons // LANES):
        block = jnp.concatenate([top, cells[:, g * LANES : (g + 1) * LANES], *sums], axis=0).astype(BF)
        send[g * share : (g + 1) * share, start:, :] = jnp.broadcast_to(block[None], (share, SUBLANES, LANES))


def step_kernel(got, mode_filter, send, weights, stacked, grads, aux, *, items, k_in, k_out, lons):
    lats, levs = got.shape[0], got.shape[1]
    block = (LANES, LANES)
    lat_total = LANES // SUBLANES
    half_in, half_out = k_in // 2, k_out // 2
    at_weights = SUBLANES * (items + 1)
    at_aux = at_weights + half_in + half_out
    hiddens = 2 * LANES
    lane, row = lane_index(block), row_index(block)

    for p in range(2):
        columns = slice(p * LANES, (p + 1) * LANES)
        for lat in range(lats):
            one = got[lat, 2 * p, at_weights:at_aux, :].astype(F32)
            two = got[lat, 2 * p + 1, at_weights:at_aux, :].astype(F32)
            top, bottom = halves(one, two)
            a, b = lat * k_in, lats * k_in + lat * k_out
            weights[a : a + k_in, columns] = jnp.concatenate([top[:half_in], bottom[:half_in]], axis=0).astype(BF)
            weights[b : b + k_out, columns] = jnp.concatenate([top[half_in:], bottom[half_in:]], axis=0).astype(BF)
    taps = lats * k_in

    sums = jnp.zeros((4, LANES), F32)
    for lev in range(levs):
        total = got[0, lev, at_aux + 4 : at_aux + 8, :].astype(F32)
        for lat in range(1, lats):
            total = total + got[lat, lev, at_aux + 4 : at_aux + 8, :].astype(F32)
        sums = sums + jnp.where(lane_index(total.shape) // 32 == lev, total, 0.0)
    scale = [
        lax.rsqrt((sums[2 * m : 2 * m + 1] + sums[2 * m + 1 : 2 * m + 2]) / (lat_total * lons) + 1e-05)
        for m in range(2)
    ]

    def spread(first):
        return jnp.concatenate(
            [
                jnp.broadcast_to(got[lat, 0, at_aux + first + n : at_aux + first + n + 1, :].astype(F32), (SUBLANES, LANES))
                for lat in range(lats)
                for n in range(2)
            ],
            axis=0,
        )

    basis_rows, mask_rows = spread(0), spread(2)
    device = lax.axis_index("lat") * levs + lax.axis_index("lev")
    own = lane == device % lat_total * SUBLANES + row % SUBLANES
    mask = jnp.dot(jnp.where(own, mask_rows, 0.0).astype(BF), jnp.ones(block, BF), preferred_element_type=F32)
    latitude = (row // SUBLANES).astype(F32)
    cosine = jnp.cos((latitude + 0.5) * (math.pi / lat_total) - 0.5 * math.pi)
    weight_sum = jnp.sum(jnp.where(lane == LANES - 1, cosine * basis_rows, 0.0)) / SUBLANES
    normaliser = items * LANES * weight_sum
    cell_weight = cosine * mask
    cell_scale = cell_weight / normaliser

    modes = mode_filter.shape[1]
    aux[...] = jnp.zeros_like(aux)
    aux[0:1, 0:modes] = mode_filter[...]
    basis = jnp.where(lane < modes, basis_rows, 0.0)
    operator = lax.dot_general(basis * aux[0:1, :], basis, NT, precision=HIGHEST)
    operator = jnp.where(row % SUBLANES == lane % SUBLANES, operator, 0.0)
    high = operator.astype(BF)
    operator = jnp.concatenate([high, (operator - high.astype(F32)).astype(BF)], axis=1)

    def spectral(v):
        return jnp.dot(operator, jnp.concatenate([v, v], axis=0), preferred_element_type=F32)

    def field_pair(group):
        at = slice(group * SUBLANES, (group + 1) * SUBLANES)
        parts = quarters([got[:, lev, at, :].astype(F32).reshape(lats * SUBLANES, LANES) for lev in range(levs)])
        parts = [q.reshape(lats, 1, SUBLANES, LANES) for q in parts]
        return [jnp.concatenate(parts[2 * k : 2 * k + 2], axis=1).reshape(block) for k in range(2)]

    states = [f for g in range(items // 2) for f in field_pair(g)]
    targets = [f for g in range(items // 2, items) for f in field_pair(g)]
    scaled = [NOISE_SCALE * (f * scale[m]) for m, f in enumerate(field_pair(items))]
    edge = jnp.zeros((SUBLANES, LANES), F32)

    def shifted(x, axis_rows=SUBLANES):
        zeros = jnp.zeros((axis_rows, x.shape[1]), F32)
        return jnp.concatenate([zeros, x[:-axis_rows]], axis=0), jnp.concatenate([x[axis_rows:], zeros], axis=0)

    for item in range(items):
        for m in range(2):
            x = (states[item] + scaled[m]).astype(BF).astype(F32)
            before, after = shifted(x)
            at = (2 * item + m) * LANES
            stacked[at : at + LANES, :] = jnp.concatenate([before, x, after], axis=1).astype(BF)

    first = weights[0:taps, :]
    second = weights[taps:, :]
    loss = jnp.zeros(block, F32)
    for item in range(items):
        at = slice(2 * item * LANES, 2 * (item + 1) * LANES)
        x = stacked[at, :]
        pre_act = jnp.dot(x, first, preferred_element_type=F32)
        sigmoid = jax.nn.sigmoid(pre_act)
        hidden = (pre_act * sigmoid).astype(BF)
        slope = sigmoid * (1.0 + pre_act * (1.0 - sigmoid))
        branch = lax.dot_general(hidden, second, NT, preferred_element_type=F32).astype(BF)
        base = states[item]
        d_one = base + spectral(branch[:LANES]) - targets[item]
        d_two = base + spectral(branch[LANES:]) - targets[item]
        loss = loss + (0.375 * (d_one * d_one + d_two * d_two) + 0.25 * d_one * d_two)
        g_one = (cell_scale * (0.75 * d_one + 0.25 * d_two)).astype(BF)
        g_two = (cell_scale * (0.75 * d_two + 0.25 * d_one)).astype(BF)
        g_branch = jnp.concatenate([spectral(g_one), spectral(g_two)], axis=0).astype(BF)
        g_hidden = jnp.dot(g_branch, second, preferred_element_type=F32)
        g_pre = (g_hidden * slope).astype(BF)
        part_in = lax.dot_general(x, g_pre, TN, preferred_element_type=F32)
        part_out = lax.dot_general(g_branch, hidden, TN, preferred_element_type=F32)
        if item == 0:
            grads[0:taps, :] = part_in
            grads[taps:, :] = part_out
        else:
            grads[0:taps, :] += part_in
            grads[taps:, :] += part_out

    loss_part = jnp.sum(loss * cell_weight, keepdims=True) / normaliser
    terms = []
    for _ in range(3):
        term = loss_part.astype(BF).astype(F32)
        terms.append(jnp.broadcast_to(term, (1, LANES)))
        loss_part = loss_part - term
    terms.append(jnp.zeros((SUBLANES - 3, LANES), F32))
    terms = jnp.concatenate(terms, axis=0)
    for p in range(2):
        columns = slice(p * LANES, (p + 1) * LANES)
        for lat in range(lats):
            a, b = lat * k_in, taps + lat * k_out
            top = jnp.concatenate([grads[a : a + half_in, columns], grads[b : b + half_out, columns]], axis=0)
            bottom = jnp.concatenate(
                [grads[a + half_in : a + k_in, columns], grads[b + half_out : b + k_out, columns]], axis=0
            )
            for lev, part in zip((2 * p, 2 * p + 1), halves(top, bottom)):
                send[lat * levs + lev] = jnp.concatenate([part, terms], axis=0).astype(BF)


def update_kernel(got, w_in, m_in, v_in, w_out, m_out, v_out, loss, nw_in, nm_in, nv_in, nw_out, nm_out, nv_out):
    total = jnp.sum(got[...].astype(F32), axis=0)
    half_in, half_out = w_in.shape[0] // 2, w_out.shape[0] // 2
    at_loss = half_in + half_out

    def unfolded(rows):
        return jnp.concatenate([rows[:, : LANES // 2], rows[:, LANES // 2 :]], axis=0)

    new = adamw(w_in[...], m_in[...], v_in[...], unfolded(total[:half_in]))
    nw_in[...], nm_in[...], nv_in[...] = new
    new = adamw(w_out[...], m_out[...], v_out[...], unfolded(total[half_in:at_loss]))
    nw_out[...], nm_out[...], nv_out[...] = new
    loss[...] = jnp.sum(total[at_loss:, :1], axis=0, keepdims=True)


def kernel_body(state, target, noise, mask, basis, mode_filter, w_in, w_out, m_in, v_in, m_out, v_out):
    items, _, _, lons = state.shape
    lats, levs = lax.axis_size("lat"), lax.axis_size("lev")
    devices = lats * levs
    k_in, k_out = w_in.shape[0], w_out.shape[1]
    rows = SUBLANES * (items + 1) + (k_in + k_out) // 2 + SUBLANES
    back_rows = (k_in + k_out) // 2 + SUBLANES

    def shape(dims, kind=F32):
        return jax.ShapeDtypeStruct(dims, kind)

    send = pl.pallas_call(
        pack_kernel,
        out_shape=shape((devices, rows, LANES), BF),
        scratch_shapes=[pltpu.VMEM((SUBLANES, LANES), F32)],
        name="pack",
    )(
        state.reshape(-1, lons),
        target.reshape(-1, lons),
        noise.reshape(-1, lons),
        mask,
        basis,
        w_in,
        w_out.T,
    )
    got = lax.all_to_all(send, EVERY, 0, 0, tiled=True)

    def step(*refs):
        step_kernel(*refs, items=items, k_in=k_in, k_out=k_out, lons=lons)

    inputs = lats * (k_in + k_out)
    back = pl.pallas_call(
        step,
        out_shape=shape((devices, back_rows, LANES), BF),
        scratch_shapes=[
            pltpu.VMEM((inputs, 2 * LANES), BF),
            pltpu.VMEM((2 * items * LANES, 3 * LANES), BF),
            pltpu.VMEM((inputs, 2 * LANES), F32),
            pltpu.VMEM((SUBLANES, LANES), F32),
        ],
        name="step",
    )(got.reshape(lats, levs, rows, LANES), mode_filter[None])
    back = lax.all_to_all(back, EVERY, 0, 0, tiled=True)
    wide, tall = shape(w_in.shape), shape(w_out.shape[::-1])
    loss, *new = pl.pallas_call(
        update_kernel,
        out_shape=(shape((1, 1)), wide, wide, wide, tall, tall, tall),
        name="update",
    )(back, w_in, m_in, v_in, w_out.T, m_out.T, v_out.T)
    return (loss.reshape(()), *new[:3], *[n.T for n in new[3:]])


def solution(mesh):
    field = P(None, "lat", "lev", None)
    row, first, second = P("lat", None), P("lat", "lev"), P("lev", "lat")
    lats, levs = mesh.shape["lat"], mesh.shape["lev"]

    def body(*arrays):
        step = kernel_body if kernels_fit(arrays, lats, levs) else plain_body
        return step(*arrays)

    return jax.shard_map(
        body,
        mesh=mesh,
        in_specs=(field, field, field, row, row, P(), first, second, first, first, second, second),
        out_specs=(P(), first, first, first, second, second, second),
        check_vma=False,
    )
```

```python
import math

import jax
import jax.numpy as jnp
from jax import lax
from jax.experimental import pallas as pl
from jax.experimental.pallas import tpu as pltpu
from jax.sharding import PartitionSpec as P

STEP = 7
NOISE_SCALE = 0.5
LEARN_RATE = 0.02
BETA_ONE = 0.9
BETA_TWO = 0.95
EPSILON = 1e-08
WEIGHT_DECAY = 0.1
EVERY = ("lat", "lev")
BF = jnp.bfloat16
F32 = jnp.float32


def adamw(weight, moment_one, moment_two, gradient):
    moment_one = BETA_ONE * moment_one + (1.0 - BETA_ONE) * gradient
    moment_two = BETA_TWO * moment_two + (1.0 - BETA_TWO) * gradient * gradient
    fix_one = 1.0 - BETA_ONE**STEP
    fix_two = 1.0 - BETA_TWO**STEP
    update = moment_one / fix_one / (jnp.sqrt(moment_two / fix_two) + EPSILON)
    return (weight - LEARN_RATE * (update + WEIGHT_DECAY * weight), moment_one, moment_two)


def parts_of(value, count):
    terms = []
    for _ in range(count):
        term = value.astype(BF)
        terms.append(term)
        value = value - lax.optimization_barrier(term).astype(F32)
    return terms


def exchange(pieces, devices):
    flat = jnp.concatenate([p.reshape(devices, -1) for p in pieces], axis=1)
    size = flat.shape[1]
    flat = jnp.pad(flat, ((0, 0), (0, -size % 1024)))
    flat = lax.all_to_all(flat.reshape(devices, -1, 128), EVERY, 0, 0, tiled=True).reshape(devices, -1)
    out, start = [], 0
    for p in pieces:
        count = math.prod(p.shape[1:])
        out.append(lax.slice_in_dim(flat, start, start + count, axis=1).reshape(p.shape))
        start += count
    return out


def plain_body(
    column_state,
    column_target,
    member_noise,
    land_mask,
    legendre_basis,
    mode_filter,
    weight_in,
    weight_out,
    moment_in,
    second_in,
    moment_out,
    second_out,
):
    items, rows, feats, lons = column_state.shape
    members = member_noise.shape[0]
    lats, levs = lax.axis_size("lat"), lax.axis_size("lev")
    devices = lats * levs
    lat_total, all_feats, own = lats * rows, levs * feats, lons // devices
    modes = legendre_basis.shape[1]

    def cut(field):
        field = jnp.moveaxis(field.astype(BF), -1, 0)
        return field.reshape((devices, own) + field.shape[1:])

    def every(value):
        return jnp.broadcast_to(value[None], (devices,) + value.shape)

    def whole(field):
        field = field.reshape(lats, levs, own, -1, rows, feats)
        return field.transpose(3, 0, 4, 2, 1, 5).reshape(-1, lat_total, own, all_feats)

    squares = jnp.sum(member_noise * member_noise, axis=(1, 3))
    mask_count = jnp.sum(land_mask, axis=1).astype(F32)
    got = exchange(
        [
            cut(column_state),
            cut(column_target),
            cut(member_noise),
            cut(land_mask),
            *[every(s) for s in parts_of(squares, 3)],
            every(mask_count.astype(BF)),
            every(legendre_basis.astype(BF)),
            every(weight_in.astype(BF)),
            every(weight_out.astype(BF)),
        ],
        devices,
    )
    state = whole(got[0]).astype(F32)
    target = whole(got[1]).astype(F32)
    noise = whole(got[2]).astype(F32)
    mask = got[3].reshape(lats, levs, own, rows)[:, 0].transpose(0, 2, 1).reshape(lat_total, own).astype(F32)
    squares = sum(g.astype(F32) for g in got[4:7]).reshape(lats, levs, members, feats).sum(0)
    power = squares.transpose(1, 0, 2).reshape(members, all_feats) / (lat_total * lons)
    counts = got[7].reshape(lats, levs, rows)[:, 0].reshape(lat_total).astype(F32)
    basis = got[8].reshape(lats, levs, rows, modes)[:, 0].reshape(lat_total, modes)
    full_in = got[9].reshape(lats, levs, *weight_in.shape).transpose(0, 2, 1, 3).reshape(3 * all_feats, -1)
    full_out = got[10].reshape(lats, levs, *weight_out.shape).transpose(1, 2, 0, 3).reshape(-1, all_feats)

    cosine = jnp.cos((jnp.arange(lat_total, dtype=F32) + 0.5) * (math.pi / lat_total) - 0.5 * math.pi)
    cell_weight = cosine[:, None] * mask
    normaliser = items * all_feats * jnp.sum(cosine * counts)

    scaled = noise * lax.rsqrt(power + 1e-05)[:, None, None, :]
    inputs = (state[:, None] + NOISE_SCALE * scaled[None]).astype(BF)
    padded = jnp.pad(inputs, ((0, 0), (0, 0), (1, 1), (0, 0), (0, 0)))
    stacked = jnp.concatenate([padded[:, :, t : t + lat_total] for t in range(3)], axis=-1)

    def spectral(field):
        coefficients = jnp.einsum("nk,imnlf->imklf", basis, field, preferred_element_type=F32)
        filtered = (mode_filter[:, None, None] * coefficients).astype(BF)
        return jnp.einsum("nk,imklf->imnlf", basis, filtered, preferred_element_type=F32)

    pre_act = jnp.einsum("imnlc,ch->imnlh", stacked, full_in, preferred_element_type=F32)
    hidden = jax.nn.silu(pre_act).astype(BF)
    branch = jnp.einsum("imnlh,hf->imnlf", hidden, full_out, preferred_element_type=F32).astype(BF)
    prediction = state[:, None] + spectral(branch)
    d_one = prediction[:, 0] - target
    d_two = prediction[:, 1] - target
    error_cell = 0.375 * (d_one * d_one + d_two * d_two) + 0.25 * d_one * d_two
    loss_part = jnp.sum(cell_weight[None, :, :, None] * error_cell) / normaliser
    cell_scale = cell_weight[None, :, :, None] / normaliser
    g_one = cell_scale * (0.75 * d_one + 0.25 * d_two)
    g_two = cell_scale * (0.75 * d_two + 0.25 * d_one)
    g_pred = jnp.stack([g_one, g_two], axis=1).astype(BF)
    g_branch = spectral(g_pred).astype(BF)
    g_hidden = jnp.einsum("imnlf,hf->imnlh", g_branch, full_out, preferred_element_type=F32)
    sigmoid = jax.nn.sigmoid(pre_act)
    g_pre = (g_hidden * sigmoid * (1.0 + pre_act * (1.0 - sigmoid))).astype(BF)
    grad_in = jnp.einsum("imnlc,imnlh->ch", stacked, g_pre, preferred_element_type=F32)
    grad_out = jnp.einsum("imnlh,imnlf->hf", hidden, g_branch, preferred_element_type=F32)

    k_in, h_in = weight_in.shape
    h_out, f_out = weight_out.shape
    back = exchange(
        [
            grad_in.astype(BF).reshape(lats, k_in, levs, h_in).transpose(0, 2, 1, 3).reshape(devices, -1),
            grad_out.astype(BF).reshape(levs, h_out, lats, f_out).transpose(2, 0, 1, 3).reshape(devices, -1),
            *[every(t[None]) for t in parts_of(loss_part, 3)],
        ],
        devices,
    )
    grad_in = jnp.sum(back[0].astype(F32), axis=0).reshape(k_in, h_in)
    grad_out = jnp.sum(back[1].astype(F32), axis=0).reshape(h_out, f_out)
    loss_value = sum(jnp.sum(b.astype(F32)) for b in back[2:5])
    new_in = adamw(weight_in, moment_in, second_in, grad_in)
    new_out = adamw(weight_out, moment_out, second_out, grad_out)
    return (loss_value, *new_in, *new_out)


LANES = 128
SUBLANES = 8
NT = (((1,), (1,)), ((), ()))
TN = (((0,), (0,)), ((), ()))
HIGHEST = lax.Precision.HIGHEST


def kernels_fit(arrays, lats, levs):
    items, rows, feats, lons = arrays[0].shape
    members, modes = arrays[2].shape[0], arrays[4].shape[1]
    devices = lats * levs
    return (
        lons == devices * SUBLANES
        and lats * rows * SUBLANES == LANES
        and (rows, feats, levs, members) == (2, LANES // 4, 4, 2)
        and items % 2 == 0
        and lons % LANES == 0
        and modes < LANES
        and arrays[6].shape[0] % 16 == 0
        and arrays[7].shape[1] % 16 == 0
        and arrays[6].shape[1] == arrays[7].shape[0] == LANES // 2
    )


def lane_index(shape):
    return lax.broadcasted_iota(jnp.int32, shape, len(shape) - 1)


def row_index(shape):
    return lax.broadcasted_iota(jnp.int32, shape, len(shape) - 2)


def halves(top, bottom):
    first = lane_index(top.shape) < LANES // 2
    turned_top, turned_bottom = pltpu.roll(top, LANES // 2, 1), pltpu.roll(bottom, LANES // 2, 1)
    return jnp.where(first, top, turned_bottom), jnp.where(first, turned_top, bottom)


def quarters(v):
    a0, a2 = halves(v[0], v[2])
    a1, a3 = halves(v[1], v[3])
    even = lane_index(a0.shape) // 32 % 2 == 0

    def pair(a, b):
        return jnp.where(even, a, pltpu.roll(b, 32, 1)), jnp.where(even, pltpu.roll(a, 96, 1), b)

    return (*pair(a0, a1), *pair(a2, a3))


def pack_kernel(*refs):
    sources, send, arrivals, (aux, arrived) = refs[:7], refs[7], refs[8:15], refs[15:]
    copies = [pltpu.make_async_copy(s, a, arrived.at[n]) for n, (s, a) in enumerate(zip(sources, arrivals))]
    for copy in copies:
        copy.start()
    state, target, noise, mask, basis, first, second = arrivals
    devices, lons = send.shape[0], state.shape[1]
    eye = (row_index((lons, lons)) == lane_index((lons, lons))).astype(BF)

    def turned(rows):
        out = lax.dot_general(eye, rows.astype(BF), NT, preferred_element_type=F32)
        return [out[:, g : g + LANES].reshape(devices, SUBLANES, LANES) for g in range(0, out.shape[1], LANES)]

    for copy in copies:
        copy.wait()
    fields = noise[...]
    groups = turned(state[...]) + turned(target[...]) + turned(fields)
    start = SUBLANES * len(groups)
    send[:, :start, :] = jnp.concatenate(groups, axis=1).astype(BF)

    def folded(rows):
        half = rows.shape[0] // 2
        return jnp.concatenate([rows[:half], rows[half:]], axis=1)

    weights = jnp.concatenate([folded(first[...]), folded(second[...])], axis=0).astype(BF)
    send[:, start : start + weights.shape[0], :] = jnp.broadcast_to(weights[None], (devices,) + weights.shape)
    start += weights.shape[0]

    squares = lax.dot_general(jnp.ones((SUBLANES, lons), F32), fields * fields, NT, precision=HIGHEST)
    count = squares.shape[1]
    source, feature = row_index((count, LANES)), lane_index((count, LANES)) % 32
    sums = []
    for member in range(2):
        pick = ((source // 64 == member) & (source % 32 == feature)).astype(F32)
        total = jnp.dot(squares, pick, precision=HIGHEST)
        high = total.astype(BF).astype(F32)
        sums += [high[:1], (total - high)[:1]]
    cells = mask[...].astype(F32)
    aux[...] = jnp.zeros_like(aux)
    aux[0:2, 0 : basis.shape[1]] = basis[...]
    counts = jnp.sum(cells, axis=1, keepdims=True)
    top = aux[0:2, :]
    top = jnp.where(lane_index(top.shape) == LANES - 1, counts, top)
    share = LANES // SUBLANES
    for g in range(lons // LANES):
        block = jnp.concatenate([top, cells[:, g * LANES : (g + 1) * LANES], *sums], axis=0).astype(BF)
        send[g * share : (g + 1) * share, start:, :] = jnp.broadcast_to(block[None], (share, SUBLANES, LANES))


def step_kernel(got, mode_filter, send, weights, stacked, hiddens, slopes, grads, aux, arrived, *, items, k_in, k_out, lons, modes):
    filter_copy = pltpu.make_async_copy(mode_filter, aux.at[0:1, :], arrived)
    filter_copy.start()
    lats, levs = got.shape[0], got.shape[1]
    block = (LANES, LANES)
    lat_total = LANES // SUBLANES
    half_in, half_out = k_in // 2, k_out // 2
    at_weights = SUBLANES * (items + 1)
    at_aux = at_weights + half_in + half_out
    lane, row = lane_index(block), row_index(block)

    for p in range(2):
        columns = slice(p * LANES, (p + 1) * LANES)
        for lat in range(lats):
            one = got[lat, 2 * p, at_weights:at_aux, :].astype(F32)
            two = got[lat, 2 * p + 1, at_weights:at_aux, :].astype(F32)
            top, bottom = halves(one, two)
            a, b = lat * k_in, lats * k_in + lat * k_out
            weights[a : a + k_in, columns] = jnp.concatenate([top[:half_in], bottom[:half_in]], axis=0).astype(BF)
            weights[b : b + k_out, columns] = jnp.concatenate([top[half_in:], bottom[half_in:]], axis=0).astype(BF)
    taps = lats * k_in

    sums = jnp.zeros((4, LANES), F32)
    for lev in range(levs):
        total = got[0, lev, at_aux + 4 : at_aux + 8, :].astype(F32)
        for lat in range(1, lats):
            total = total + got[lat, lev, at_aux + 4 : at_aux + 8, :].astype(F32)
        sums = sums + jnp.where(lane_index(total.shape) // 32 == lev, total, 0.0)
    scale = [
        lax.rsqrt((sums[2 * m : 2 * m + 1] + sums[2 * m + 1 : 2 * m + 2]) / (lat_total * lons) + 1e-05)
        for m in range(2)
    ]

    def spread(rows):
        return jnp.concatenate([jnp.broadcast_to(r, (SUBLANES, LANES)) for r in rows], axis=0)

    tops = [got[lat, 0, at_aux : at_aux + 4, :].astype(F32) for lat in range(lats)]
    basis_rows = spread([t[n : n + 1] for t in tops for n in range(2)])
    mask_rows = spread([t[n : n + 1] for t in tops for n in range(2, 4)])
    device = lax.axis_index("lat") * levs + lax.axis_index("lev")
    own = lane == device % lat_total * SUBLANES + row % SUBLANES
    mask = jnp.dot(jnp.where(own, mask_rows, 0.0).astype(BF), jnp.ones(block, BF), preferred_element_type=F32)
    latitude = row_index((lat_total, LANES)).astype(F32)
    cosine = jnp.cos((latitude + 0.5) * (math.pi / lat_total) - 0.5 * math.pi)
    cosine = spread([cosine[n : n + 1] for n in range(lat_total)])
    weight_sum = jnp.sum(jnp.where(lane == LANES - 1, cosine * basis_rows, 0.0)) / SUBLANES
    normaliser = items * LANES * weight_sum
    cell_weight = cosine * mask
    cell_scale = cell_weight / normaliser

    basis = jnp.where(lane < modes, basis_rows, 0.0)
    filter_copy.wait()
    factors = jnp.where(lane_index((1, LANES)) < modes, aux[0:1, :], 0.0)
    operator = lax.dot_general(basis * factors, basis, NT, precision=HIGHEST)
    operator = jnp.where(row % SUBLANES == lane % SUBLANES, operator, 0.0)
    high = operator.astype(BF)
    operator = jnp.concatenate([high, (operator - high.astype(F32)).astype(BF)], axis=1)

    def spectral(v):
        return jnp.dot(operator, jnp.concatenate([v, v], axis=0), preferred_element_type=F32)

    def field_pair(group):
        at = slice(group * SUBLANES, (group + 1) * SUBLANES)
        parts = quarters([got[:, lev, at, :].astype(F32).reshape(lats * SUBLANES, LANES) for lev in range(levs)])
        parts = [q.reshape(lats, 1, SUBLANES, LANES) for q in parts]
        return [jnp.concatenate(parts[2 * k : 2 * k + 2], axis=1).reshape(block) for k in range(2)]

    states = [f for g in range(items // 2) for f in field_pair(g)]
    targets = [f for g in range(items // 2, items) for f in field_pair(g)]
    scaled = [NOISE_SCALE * (f * scale[m]) for m, f in enumerate(field_pair(items))]
    edge = jnp.zeros((SUBLANES, LANES), F32)

    def shifted(x, axis_rows=SUBLANES):
        zeros = jnp.zeros((axis_rows, x.shape[1]), F32)
        return jnp.concatenate([zeros, x[:-axis_rows]], axis=0), jnp.concatenate([x[axis_rows:], zeros], axis=0)

    for item in range(items):
        for m in range(2):
            x = (states[item] + scaled[m]).astype(BF).astype(F32)
            before, after = shifted(x)
            at = (2 * item + m) * LANES
            stacked[at : at + LANES, :] = jnp.concatenate([before, x, after], axis=1).astype(BF)

    first = weights[0:taps, :]
    second = weights[taps:, :]
    spans = [slice(2 * item * LANES, 2 * (item + 1) * LANES) for item in range(items)]
    branches, gradients, errors = {}, {}, []

    def forward(item):
        pre_act = jnp.dot(stacked[spans[item], :], first, preferred_element_type=F32)
        sigmoid = jax.nn.sigmoid(pre_act)
        hidden = (pre_act * sigmoid).astype(BF)
        hiddens[spans[item], :] = hidden
        slopes[spans[item], :] = sigmoid * (1.0 + pre_act * (1.0 - sigmoid))
        branches[item] = lax.dot_general(hidden, second, NT, preferred_element_type=F32).astype(BF)

    def compare(item):
        branch, base = branches[item], states[item]
        d_one = base + spectral(branch[:LANES]) - targets[item]
        d_two = base + spectral(branch[LANES:]) - targets[item]
        errors.append(0.375 * (d_one * d_one + d_two * d_two) + 0.25 * d_one * d_two)
        g_one = (cell_scale * (0.75 * d_one + 0.25 * d_two)).astype(BF)
        g_two = (cell_scale * (0.75 * d_two + 0.25 * d_one)).astype(BF)
        gradients[item] = jnp.concatenate([spectral(g_one), spectral(g_two)], axis=0).astype(BF)

    def backward(item):
        g_hidden = jnp.dot(gradients[item], second, preferred_element_type=F32)
        g_pre = (g_hidden * slopes[spans[item], :]).astype(BF)
        part_in = lax.dot_general(stacked[spans[item], :], g_pre, TN, preferred_element_type=F32)
        part_out = lax.dot_general(gradients[item], hiddens[spans[item], :], TN, preferred_element_type=F32)
        if item == 0:
            grads[0:taps, :] = part_in
            grads[taps:, :] = part_out
        else:
            grads[0:taps, :] += part_in
            grads[taps:, :] += part_out

    stages = (forward, compare, backward)
    for turn in range(items + len(stages) - 1):
        for late, stage in enumerate(stages):
            if 0 <= turn - late < items:
                stage(turn - late)
    loss = sum(errors[1:], errors[0])

    loss_part = jnp.sum(loss * cell_weight, keepdims=True) / normaliser
    terms = []
    for _ in range(3):
        term = loss_part.astype(BF).astype(F32)
        terms.append(jnp.broadcast_to(term, (1, LANES)))
        loss_part = loss_part - term
    terms.append(jnp.zeros((SUBLANES - 3, LANES), F32))
    terms = jnp.concatenate(terms, axis=0)
    for p in range(2):
        columns = slice(p * LANES, (p + 1) * LANES)
        for lat in range(lats):
            a, b = lat * k_in, taps + lat * k_out
            top = jnp.concatenate([grads[a : a + half_in, columns], grads[b : b + half_out, columns]], axis=0)
            bottom = jnp.concatenate(
                [grads[a + half_in : a + k_in, columns], grads[b + half_out : b + k_out, columns]], axis=0
            )
            for lev, part in zip((2 * p, 2 * p + 1), halves(top, bottom)):
                send[lat * levs + lev] = jnp.concatenate([part, terms], axis=0).astype(BF)


def update_kernel(got, w_in, m_in, v_in, w_out, m_out, v_out, loss, nw_in, nm_in, nv_in, nw_out, nm_out, nv_out):
    total = jnp.sum(got[...].astype(F32), axis=0)
    half_in, half_out = w_in.shape[0] // 2, w_out.shape[0] // 2
    at_loss = half_in + half_out

    def unfolded(rows):
        return jnp.concatenate([rows[:, : LANES // 2], rows[:, LANES // 2 :]], axis=0)

    new = adamw(w_in[...], m_in[...], v_in[...], unfolded(total[:half_in]))
    nw_in[...], nm_in[...], nv_in[...] = new
    new = adamw(w_out[...], m_out[...], v_out[...], unfolded(total[half_in:at_loss]))
    nw_out[...], nm_out[...], nv_out[...] = new
    loss[...] = jnp.sum(total[at_loss:, :1], axis=0, keepdims=True)


def kernel_body(state, target, noise, mask, basis, mode_filter, w_in, w_out, m_in, v_in, m_out, v_out):
    items, _, _, lons = state.shape
    lats, levs = lax.axis_size("lat"), lax.axis_size("lev")
    devices = lats * levs
    k_in, k_out = w_in.shape[0], w_out.shape[1]
    rows = SUBLANES * (items + 1) + (k_in + k_out) // 2 + SUBLANES
    back_rows = (k_in + k_out) // 2 + SUBLANES

    def shape(dims, kind=F32):
        return jax.ShapeDtypeStruct(dims, kind)

    sources = (
        state.reshape(-1, lons),
        target.reshape(-1, lons),
        noise.reshape(-1, lons),
        mask,
        basis,
        w_in,
        w_out.T,
    )
    send = pl.pallas_call(
        pack_kernel,
        out_shape=shape((devices, rows, LANES), BF),
        in_specs=[pl.BlockSpec(memory_space=pltpu.HBM)] * len(sources),
        scratch_shapes=[
            *[pltpu.VMEM(s.shape, s.dtype) for s in sources],
            pltpu.VMEM((SUBLANES, LANES), F32),
            pltpu.SemaphoreType.DMA((len(sources),)),
        ],
        name="pack",
    )(*sources)
    got = lax.all_to_all(send, EVERY, 0, 0, tiled=True)

    def step(*refs):
        step_kernel(*refs, items=items, k_in=k_in, k_out=k_out, lons=lons, modes=modes)

    inputs, cells, modes = lats * (k_in + k_out), 2 * items * LANES, basis.shape[1]
    padded_filter = jnp.pad(mode_filter[None], ((0, 0), (0, LANES - modes)))
    back = pl.pallas_call(
        step,
        out_shape=shape((devices, back_rows, LANES), BF),
        scratch_shapes=[
            pltpu.VMEM((inputs, 2 * LANES), BF),
            pltpu.VMEM((cells, 3 * LANES), BF),
            pltpu.VMEM((cells, 2 * LANES), BF),
            pltpu.VMEM((cells, 2 * LANES), F32),
            pltpu.VMEM((inputs, 2 * LANES), F32),
            pltpu.VMEM((SUBLANES, LANES), F32),
            pltpu.SemaphoreType.DMA,
        ],
        in_specs=[pl.BlockSpec(memory_space=pltpu.VMEM), pl.BlockSpec(memory_space=pltpu.HBM)],
        compiler_params=pltpu.CompilerParams(vmem_limit_bytes=16 * 2**20),
        name="step",
    )(got.reshape(lats, levs, rows, LANES), padded_filter)
    back = lax.all_to_all(back, EVERY, 0, 0, tiled=True)
    wide, tall = shape(w_in.shape), shape(w_out.shape[::-1])
    loss, *new = pl.pallas_call(
        update_kernel,
        out_shape=(shape((1, 1)), wide, wide, wide, tall, tall, tall),
        compiler_params=pltpu.CompilerParams(vmem_limit_bytes=8 * 2**20),
        name="update",
    )(back, w_in, m_in, v_in, w_out.T, m_out.T, v_out.T)
    return (loss.reshape(()), *new[:3], *[n.T for n in new[3:]])


def solution(mesh):
    field = P(None, "lat", "lev", None)
    row, first, second = P("lat", None), P("lat", "lev"), P("lev", "lat")
    lats, levs = mesh.shape["lat"], mesh.shape["lev"]

    def body(*arrays):
        step = kernel_body if kernels_fit(arrays, lats, levs) else plain_body
        return step(*arrays)

    return jax.shard_map(
        body,
        mesh=mesh,
        in_specs=(field, field, field, row, row, P(), first, second, first, first, second, second),
        out_specs=(P(), first, first, first, second, second, second),
        check_vma=False,
    )
```

```python
import functools
import math

import jax
import jax.numpy as jnp
from jax import lax
from jax.experimental import pallas as pl
from jax.experimental.pallas import tpu as pltpu
from jax.sharding import PartitionSpec as P

STEP = 7
NOISE_SCALE = 0.5
LEARN_RATE = 0.02
BETA_ONE = 0.9
BETA_TWO = 0.95
EPSILON = 1e-08
WEIGHT_DECAY = 0.1
EVERY = ("lat", "lev")
BF = jnp.bfloat16
F32 = jnp.float32


def adamw(weight, moment_one, moment_two, gradient):
    moment_one = BETA_ONE * moment_one + (1.0 - BETA_ONE) * gradient
    moment_two = BETA_TWO * moment_two + (1.0 - BETA_TWO) * gradient * gradient
    fix_one = 1.0 - BETA_ONE**STEP
    fix_two = 1.0 - BETA_TWO**STEP
    update = moment_one / fix_one / (jnp.sqrt(moment_two / fix_two) + EPSILON)
    return (weight - LEARN_RATE * (update + WEIGHT_DECAY * weight), moment_one, moment_two)


def parts_of(value, count):
    terms = []
    for _ in range(count):
        term = value.astype(BF)
        terms.append(term)
        value = value - lax.optimization_barrier(term).astype(F32)
    return terms


def exchange(pieces, devices):
    flat = jnp.concatenate([p.reshape(devices, -1) for p in pieces], axis=1)
    size = flat.shape[1]
    flat = jnp.pad(flat, ((0, 0), (0, -size % 1024)))
    flat = lax.all_to_all(flat.reshape(devices, -1, 128), EVERY, 0, 0, tiled=True).reshape(devices, -1)
    out, start = [], 0
    for p in pieces:
        count = math.prod(p.shape[1:])
        out.append(lax.slice_in_dim(flat, start, start + count, axis=1).reshape(p.shape))
        start += count
    return out


def plain_body(
    column_state,
    column_target,
    member_noise,
    land_mask,
    legendre_basis,
    mode_filter,
    weight_in,
    weight_out,
    moment_in,
    second_in,
    moment_out,
    second_out,
):
    items, rows, feats, lons = column_state.shape
    members = member_noise.shape[0]
    lats, levs = lax.axis_size("lat"), lax.axis_size("lev")
    devices = lats * levs
    lat_total, all_feats, own = lats * rows, levs * feats, lons // devices
    modes = legendre_basis.shape[1]

    def cut(field):
        field = jnp.moveaxis(field.astype(BF), -1, 0)
        return field.reshape((devices, own) + field.shape[1:])

    def every(value):
        return jnp.broadcast_to(value[None], (devices,) + value.shape)

    def whole(field):
        field = field.reshape(lats, levs, own, -1, rows, feats)
        return field.transpose(3, 0, 4, 2, 1, 5).reshape(-1, lat_total, own, all_feats)

    squares = jnp.sum(member_noise * member_noise, axis=(1, 3))
    mask_count = jnp.sum(land_mask, axis=1).astype(F32)
    got = exchange(
        [
            cut(column_state),
            cut(column_target),
            cut(member_noise),
            cut(land_mask),
            *[every(s) for s in parts_of(squares, 3)],
            every(mask_count.astype(BF)),
            every(legendre_basis.astype(BF)),
            every(weight_in.astype(BF)),
            every(weight_out.astype(BF)),
        ],
        devices,
    )
    state = whole(got[0]).astype(F32)
    target = whole(got[1]).astype(F32)
    noise = whole(got[2]).astype(F32)
    mask = got[3].reshape(lats, levs, own, rows)[:, 0].transpose(0, 2, 1).reshape(lat_total, own).astype(F32)
    squares = sum(g.astype(F32) for g in got[4:7]).reshape(lats, levs, members, feats).sum(0)
    power = squares.transpose(1, 0, 2).reshape(members, all_feats) / (lat_total * lons)
    counts = got[7].reshape(lats, levs, rows)[:, 0].reshape(lat_total).astype(F32)
    basis = got[8].reshape(lats, levs, rows, modes)[:, 0].reshape(lat_total, modes)
    full_in = got[9].reshape(lats, levs, *weight_in.shape).transpose(0, 2, 1, 3).reshape(3 * all_feats, -1)
    full_out = got[10].reshape(lats, levs, *weight_out.shape).transpose(1, 2, 0, 3).reshape(-1, all_feats)

    cosine = jnp.cos((jnp.arange(lat_total, dtype=F32) + 0.5) * (math.pi / lat_total) - 0.5 * math.pi)
    cell_weight = cosine[:, None] * mask
    normaliser = items * all_feats * jnp.sum(cosine * counts)

    scaled = noise * lax.rsqrt(power + 1e-05)[:, None, None, :]
    inputs = (state[:, None] + NOISE_SCALE * scaled[None]).astype(BF)
    padded = jnp.pad(inputs, ((0, 0), (0, 0), (1, 1), (0, 0), (0, 0)))
    stacked = jnp.concatenate([padded[:, :, t : t + lat_total] for t in range(3)], axis=-1)

    def spectral(field):
        coefficients = jnp.einsum("nk,imnlf->imklf", basis, field, preferred_element_type=F32)
        filtered = (mode_filter[:, None, None] * coefficients).astype(BF)
        return jnp.einsum("nk,imklf->imnlf", basis, filtered, preferred_element_type=F32)

    pre_act = jnp.einsum("imnlc,ch->imnlh", stacked, full_in, preferred_element_type=F32)
    hidden = jax.nn.silu(pre_act).astype(BF)
    branch = jnp.einsum("imnlh,hf->imnlf", hidden, full_out, preferred_element_type=F32).astype(BF)
    prediction = state[:, None] + spectral(branch)
    d_one = prediction[:, 0] - target
    d_two = prediction[:, 1] - target
    error_cell = 0.375 * (d_one * d_one + d_two * d_two) + 0.25 * d_one * d_two
    loss_part = jnp.sum(cell_weight[None, :, :, None] * error_cell) / normaliser
    cell_scale = cell_weight[None, :, :, None] / normaliser
    g_one = cell_scale * (0.75 * d_one + 0.25 * d_two)
    g_two = cell_scale * (0.75 * d_two + 0.25 * d_one)
    g_pred = jnp.stack([g_one, g_two], axis=1).astype(BF)
    g_branch = spectral(g_pred).astype(BF)
    g_hidden = jnp.einsum("imnlf,hf->imnlh", g_branch, full_out, preferred_element_type=F32)
    sigmoid = jax.nn.sigmoid(pre_act)
    g_pre = (g_hidden * sigmoid * (1.0 + pre_act * (1.0 - sigmoid))).astype(BF)
    grad_in = jnp.einsum("imnlc,imnlh->ch", stacked, g_pre, preferred_element_type=F32)
    grad_out = jnp.einsum("imnlh,imnlf->hf", hidden, g_branch, preferred_element_type=F32)

    k_in, h_in = weight_in.shape
    h_out, f_out = weight_out.shape
    back = exchange(
        [
            grad_in.astype(BF).reshape(lats, k_in, levs, h_in).transpose(0, 2, 1, 3).reshape(devices, -1),
            grad_out.astype(BF).reshape(levs, h_out, lats, f_out).transpose(2, 0, 1, 3).reshape(devices, -1),
            *[every(t[None]) for t in parts_of(loss_part, 3)],
        ],
        devices,
    )
    grad_in = jnp.sum(back[0].astype(F32), axis=0).reshape(k_in, h_in)
    grad_out = jnp.sum(back[1].astype(F32), axis=0).reshape(h_out, f_out)
    loss_value = sum(jnp.sum(b.astype(F32)) for b in back[2:5])
    new_in = adamw(weight_in, moment_in, second_in, grad_in)
    new_out = adamw(weight_out, moment_out, second_out, grad_out)
    return (loss_value, *new_in, *new_out)


LANES = 128
SUBLANES = 8
NT = (((1,), (1,)), ((), ()))
TN = (((0,), (0,)), ((), ()))
HIGHEST = lax.Precision.HIGHEST


def kernels_fit(arrays, lats, levs):
    items, rows, feats, lons = arrays[0].shape
    members, modes = arrays[2].shape[0], arrays[4].shape[1]
    devices = lats * levs
    return (
        lons == devices * SUBLANES
        and lats * rows * SUBLANES == LANES
        and (rows, feats, levs, members) == (2, LANES // 4, 4, 2)
        and items % 2 == 0
        and lons % LANES == 0
        and modes < LANES
        and arrays[6].shape[0] == 3 * arrays[7].shape[1]
        and arrays[7].shape[1] % 16 == 0
        and arrays[6].shape[1] == arrays[7].shape[0] == LANES // 2
    )


def lane_index(shape):
    return lax.broadcasted_iota(jnp.int32, shape, len(shape) - 1)


def row_index(shape):
    return lax.broadcasted_iota(jnp.int32, shape, len(shape) - 2)


def halves(top, bottom):
    first = lane_index(top.shape) < LANES // 2
    turned_top, turned_bottom = pltpu.roll(top, LANES // 2, 1), pltpu.roll(bottom, LANES // 2, 1)
    return jnp.where(first, top, turned_bottom), jnp.where(first, turned_top, bottom)


def quarters(v):
    a0, a2 = halves(v[0], v[2])
    a1, a3 = halves(v[1], v[3])
    even = lane_index(a0.shape) // 32 % 2 == 0

    def pair(a, b):
        return jnp.where(even, a, pltpu.roll(b, 32, 1)), jnp.where(even, pltpu.roll(a, 96, 1), b)

    return (*pair(a0, a1), *pair(a2, a3))


def pack_kernel(*refs):
    sources, send, arrivals, (aux, arrived) = refs[:8], refs[8], refs[9:17], refs[17:]
    copies = [pltpu.make_async_copy(s, a, arrived.at[n]) for n, (s, a) in enumerate(zip(sources, arrivals))]
    for copy in copies:
        copy.start()
    state, target, noise, mask, basis, mode_filter, first, second = arrivals
    devices, lons = send.shape[0], state.shape[1]
    eye = (row_index((lons, lons)) == lane_index((lons, lons))).astype(BF)

    def turned(rows):
        out = lax.dot_general(eye, rows.astype(BF), NT, preferred_element_type=F32)
        return [out[:, g : g + LANES].reshape(devices, SUBLANES, LANES) for g in range(0, out.shape[1], LANES)]

    for copy in copies:
        copy.wait()
    fields = noise[...]
    groups = turned(state[...]) + turned(target[...]) + turned(fields)
    start = SUBLANES * len(groups)
    send[:, :start, :] = jnp.concatenate(groups, axis=1).astype(BF)

    weights = jnp.concatenate([first[...], second[...]], axis=0)
    quarter = weights.shape[0] // 4
    folded = [
        jnp.concatenate([weights[q * quarter : (q + 1) * quarter, h * 32 : (h + 1) * 32] for q in range(4)], axis=1)
        for h in range(2)
    ]
    folded = jnp.stack(folded).astype(BF)
    pairs = jnp.broadcast_to(folded[None], (devices // 2,) + folded.shape)
    send[:, start : start + quarter, :] = pairs.reshape(devices, quarter, LANES)
    start += quarter

    squares = lax.dot_general(jnp.ones((SUBLANES, lons), F32), fields * fields, NT, precision=HIGHEST)
    count = squares.shape[1]
    source, at = row_index((count, LANES)), lane_index((count, LANES))
    pick = (source // 64 == at // 64) & (source % 32 == at % 32)
    total = jnp.dot(squares, pick.astype(F32), precision=HIGHEST)[:1]
    high = total.astype(BF).astype(F32)
    sums = jnp.where(lane_index(total.shape) // 32 % 2 == 0, high, total - high)
    cells = mask[...].astype(F32)
    modes = basis.shape[1]
    aux[...] = jnp.zeros_like(aux)
    aux[0:2, 0:modes] = basis[...].astype(BF).astype(F32) * jnp.sqrt(mode_filter[...])
    high = aux[0:2, :].astype(BF).astype(F32)
    low = aux[0:2, :] - high
    counts = jnp.sum(cells, axis=1, keepdims=True)
    high = jnp.where(lane_index(high.shape) == LANES - 1, counts, high)
    spare = jnp.zeros((1, LANES), F32)
    share = LANES // SUBLANES
    for g in range(lons // LANES):
        block = jnp.concatenate([high, low, cells[:, g * LANES : (g + 1) * LANES], sums, spare], axis=0).astype(BF)
        send[g * share : (g + 1) * share, start:, :] = jnp.broadcast_to(block[None], (share, SUBLANES, LANES))


def row_starts(lats, k_in, k_out, quarter):
    return [
        [lat * k_in + q * quarter for q in range(k_in // quarter)]
        + [lats * k_in + lat * k_out + q * quarter for q in range(k_out // quarter)]
        for lat in range(lats)
    ]


def unfold(half, weights, starts):
    lats, levs, quarter, _ = half.shape
    parts = quarters([half[:, lev].astype(F32).reshape(lats * quarter, LANES) for lev in range(levs)])
    for q, part in enumerate(parts):
        for lat in range(lats):
            at = starts[lat][q]
            weights[at : at + quarter, 0:LANES] = part[lat * quarter : (lat + 1) * quarter].astype(BF)


def prepare_kernel(got, stacked, fields, operators, scales, weights, *, items, k_in, k_out, lons, modes):
    lats, levs = got.shape[0], got.shape[1]
    at_aux = got.shape[2] - SUBLANES
    block = (LANES, LANES)
    lat_total = LANES // SUBLANES
    lane, row = lane_index(block), row_index(block)

    quarter = (k_in + k_out) // 4
    own_half = got[:, :, at_aux - quarter : at_aux, :]
    unfold(own_half, weights, row_starts(lats, k_in, k_out, quarter))

    sums = []
    for lev in range(levs):
        total = got[0, lev, at_aux:, :].astype(F32)
        for lat in range(1, lats):
            total = total + got[lat, lev, at_aux:, :].astype(F32)
        sums.append(total)
    sums = [s[6:7] for s in quarters(sums)]
    scale = [lax.rsqrt((sums[2 * m] + sums[2 * m + 1]) / (lat_total * lons) + 1e-05) for m in range(2)]

    def spread(rows):
        return jnp.concatenate([jnp.broadcast_to(r, (SUBLANES, LANES)) for r in rows], axis=0)

    tops = [got[lat, 0, at_aux:, :].astype(F32) for lat in range(lats)]
    high = spread([t[n : n + 1] for t in tops for n in range(2)])
    low = spread([t[n : n + 1] for t in tops for n in range(2, 4)])
    mask_rows = spread([t[n : n + 1] for t in tops for n in range(4, 6)])
    device = lax.axis_index("lat") * levs + lax.axis_index("lev")
    own = lane == device % lat_total * SUBLANES + row % SUBLANES
    mask = jnp.dot(jnp.where(own, mask_rows, 0.0).astype(BF), jnp.ones(block, BF), preferred_element_type=F32)
    latitude = row_index((lat_total, LANES)).astype(F32)
    cosine = jnp.cos((latitude + 0.5) * (math.pi / lat_total) - 0.5 * math.pi)
    cosine = spread([cosine[n : n + 1] for n in range(lat_total)])
    weight_sum = jnp.sum(jnp.where(lane == LANES - 1, cosine * high, 0.0)) / SUBLANES
    scales[...] = cosine * mask / (items * LANES * weight_sum)

    def field_pair(group):
        at = slice(group * SUBLANES, (group + 1) * SUBLANES)
        parts = quarters([got[:, lev, at, :].astype(F32).reshape(lats * SUBLANES, LANES) for lev in range(levs)])
        parts = [q.reshape(lats, 1, SUBLANES, LANES) for q in parts]
        return [jnp.concatenate(parts[2 * k : 2 * k + 2], axis=1).reshape(block) for k in range(2)]

    scaled = [NOISE_SCALE * (f * scale[m]) for m, f in enumerate(field_pair(items))]
    edge = jnp.zeros((SUBLANES, LANES), F32)
    for group in range(items):
        for k, field in enumerate(field_pair(group)):
            fields[2 * group + k] = field.astype(BF)
            if group >= items // 2:
                continue
            for m in range(2):
                x = (field + scaled[m]).astype(BF).astype(F32)
                before = jnp.concatenate([edge, x[:-SUBLANES]], axis=0)
                after = jnp.concatenate([x[SUBLANES:], edge], axis=0)
                at = (2 * (2 * group + k) + m) * LANES
                stacked[at : at + LANES, :] = jnp.concatenate([before, x, after], axis=1).astype(BF)

    root = jnp.where(lane < modes, high + low, 0.0)
    operator = lax.dot_general(root, root, NT, precision=HIGHEST)
    operator = jnp.where(row % SUBLANES == lane % SUBLANES, operator, 0.0)
    high = operator.astype(BF)
    operators[...] = jnp.concatenate([high, (operator - high.astype(F32)).astype(BF)], axis=1)


def step_kernel(
    other, stacked, fields, operators, scales, own, give, keep, losses, weights, hiddens, slopes, g_pres, grads, *, items, k_in, k_out
):
    lats, levs, quarter, _ = other.shape
    taps = lats * k_in
    starts = row_starts(lats, k_in, k_out, quarter)
    unfold(other[...], weights, starts)
    weights[:, LANES:] = own[...]

    operator, cell_scale = operators[...], scales[...]

    def spectral(v):
        return jnp.dot(operator, jnp.concatenate([v, v], axis=0), preferred_element_type=F32)

    first = weights[0:taps, :]
    second = weights[taps:, :]
    spans = [slice(2 * item * LANES, 2 * (item + 1) * LANES) for item in range(items)]
    branches, gradients, errors = {}, {}, []

    def forward(item):
        pre_act = jnp.dot(stacked[spans[item], :], first, preferred_element_type=F32)
        sigmoid = jax.nn.sigmoid(pre_act)
        hidden = (pre_act * sigmoid).astype(BF)
        hiddens[spans[item], :] = hidden
        slopes[spans[item], :] = sigmoid * (1.0 + pre_act * (1.0 - sigmoid))
        branches[item] = lax.dot_general(hidden, second, NT, preferred_element_type=F32).astype(BF)

    def compare(item):
        branch, base, target = branches[item], fields[item].astype(F32), fields[items + item].astype(F32)
        d_one = base + spectral(branch[:LANES]) - target
        d_two = base + spectral(branch[LANES:]) - target
        errors.append(0.375 * (d_one * d_one + d_two * d_two) + 0.25 * d_one * d_two)
        g_one = (cell_scale * (0.75 * d_one + 0.25 * d_two)).astype(BF)
        g_two = (cell_scale * (0.75 * d_two + 0.25 * d_one)).astype(BF)
        gradients[item] = jnp.concatenate([spectral(g_one), spectral(g_two)], axis=0).astype(BF)

    def backward(item):
        g_hidden = jnp.dot(gradients[item], second, preferred_element_type=F32)
        g_pres[spans[item], :] = (g_hidden * slopes[spans[item], :]).astype(BF)

    stages = (forward, compare, backward)
    for turn in range(items + len(stages) - 1):
        for late, stage in enumerate(stages):
            if 0 <= turn - late < items:
                stage(turn - late)
    loss = sum(errors[1:], errors[0])
    grads[0:taps, :] = lax.dot_general(stacked[...], g_pres[...], TN, preferred_element_type=F32)
    g_branch = jnp.concatenate([gradients[item] for item in range(items)], axis=0)
    grads[taps:, :] = lax.dot_general(g_branch, hiddens[...], TN, preferred_element_type=F32)

    loss_part = jnp.sum(loss * cell_scale, keepdims=True)
    terms = []
    for _ in range(3):
        term = loss_part.astype(BF).astype(F32)
        terms.append(jnp.broadcast_to(term, (1, LANES)))
        loss_part = loss_part - term
    terms.append(jnp.zeros((SUBLANES - 3, LANES), F32))
    losses[...] = jnp.concatenate(terms, axis=0).astype(BF)
    for p, half in enumerate((give, keep)):
        columns = slice(p * LANES, (p + 1) * LANES)
        parts = [
            jnp.concatenate([grads[s[q] : s[q] + quarter, columns] for s in starts], axis=0) for q in range(4)
        ]
        for lev, part in enumerate(quarters(parts)):
            half[:, lev] = part.reshape(lats, quarter, LANES).astype(half.dtype)


def join_kernel(keep, came, losses, send):
    quarter = keep.shape[2]
    total = (keep[...] + came[...].astype(F32)).astype(BF)
    send[:, :quarter, :] = total.reshape(-1, quarter, LANES)
    send[:, quarter:, :] = jnp.broadcast_to(losses[...][None], (send.shape[0], SUBLANES, LANES))


def update_kernel(got, w_in, m_in, v_in, w_out, m_out, v_out, loss, nw_in, nm_in, nv_in, nw_out, nm_out, nv_out):
    total = jnp.sum(got[...].astype(F32), axis=0)
    at_loss = total.shape[1] - SUBLANES

    def unfolded(rows):
        return jnp.concatenate([rows[:, q * 32 : (q + 1) * 32] for q in range(4)], axis=0)

    gradient = jnp.concatenate([unfolded(total[h, :at_loss]) for h in range(2)], axis=1)
    k_in = w_in.shape[0]
    nw_in[...], nm_in[...], nv_in[...] = adamw(w_in[...], m_in[...], v_in[...], gradient[:k_in])
    nw_out[...], nm_out[...], nv_out[...] = adamw(w_out[...], m_out[...], v_out[...], gradient[k_in:])
    loss[...] = jnp.sum(total[0, at_loss:, :1] + total[1, at_loss:, :1], axis=0, keepdims=True)


def kernel_body(state, target, noise, mask, basis, mode_filter, w_in, w_out, m_in, v_in, m_out, v_out):
    items, _, _, lons = state.shape
    lats, levs = lax.axis_size("lat"), lax.axis_size("lev")
    devices = lats * levs
    k_in, k_out, modes = w_in.shape[0], w_out.shape[1], basis.shape[1]
    quarter = (k_in + k_out) // 4
    at_weights = SUBLANES * (items + 1)
    rows = at_weights + quarter + SUBLANES
    inputs, cells = lats * (k_in + k_out), 2 * items * LANES
    partners = [(i, i ^ 1) for i in range(levs)]
    vmem, hbm = pl.BlockSpec(memory_space=pltpu.VMEM), pl.BlockSpec(memory_space=pltpu.HBM)
    small = pltpu.CompilerParams(vmem_limit_bytes=8 * 2**20)

    def shape(*dims, kind=F32):
        return jax.ShapeDtypeStruct(dims, kind)

    sources = (
        state.reshape(-1, lons),
        target.reshape(-1, lons),
        noise.reshape(-1, lons),
        mask,
        basis,
        mode_filter[None],
        w_in,
        w_out.T,
    )
    send = pl.pallas_call(
        pack_kernel,
        out_shape=shape(devices, rows, LANES, kind=BF),
        in_specs=[hbm] * len(sources),
        scratch_shapes=[
            *[pltpu.VMEM(s.shape, s.dtype) for s in sources],
            pltpu.VMEM((SUBLANES, LANES), F32),
            pltpu.SemaphoreType.DMA((len(sources),)),
        ],
        name="pack",
    )(*sources)
    got = lax.all_to_all(send, EVERY, 0, 0, tiled=True).reshape(lats, levs, rows, LANES)
    own = got[:, :, at_weights : at_weights + quarter]
    other = lax.ppermute(own, "lev", partners)
    prepared = pl.pallas_call(
        functools.partial(prepare_kernel, items=items, k_in=k_in, k_out=k_out, lons=lons, modes=modes),
        out_shape=(
            shape(cells, 3 * LANES, kind=BF),
            shape(2 * items, LANES, LANES, kind=BF),
            shape(LANES, 2 * LANES, kind=BF),
            shape(LANES, LANES),
            shape(inputs, LANES, kind=BF),
        ),
        in_specs=[vmem],
        compiler_params=small,
        cost_estimate=pl.CostEstimate(flops=2**22, bytes_accessed=2**22, transcendentals=0),
        name="prepare",
    )(got)
    block = (lats, levs, quarter, LANES)
    give, keep, losses = pl.pallas_call(
        functools.partial(step_kernel, items=items, k_in=k_in, k_out=k_out),
        out_shape=(shape(*block, kind=BF), shape(*block), shape(SUBLANES, LANES, kind=BF)),
        scratch_shapes=[
            pltpu.VMEM((inputs, 2 * LANES), BF),
            pltpu.VMEM((cells, 2 * LANES), BF),
            pltpu.VMEM((cells, 2 * LANES), F32),
            pltpu.VMEM((cells, 2 * LANES), BF),
            pltpu.VMEM((inputs, 2 * LANES), F32),
        ],
        compiler_params=pltpu.CompilerParams(vmem_limit_bytes=16 * 2**20),
        name="step",
    )(other, *prepared)
    came = lax.ppermute(give, "lev", partners)
    back = pl.pallas_call(
        join_kernel,
        out_shape=shape(devices, quarter + SUBLANES, LANES, kind=BF),
        compiler_params=small,
        name="join",
    )(keep, came, losses)
    back = lax.all_to_all(back, EVERY, 0, 0, tiled=True)
    wide, tall = shape(*w_in.shape), shape(*w_out.shape[::-1])
    loss, *new = pl.pallas_call(
        update_kernel,
        out_shape=(shape(1, 1), wide, wide, wide, tall, tall, tall),
        compiler_params=small,
        name="update",
    )(back.reshape(-1, 2, quarter + SUBLANES, LANES), w_in, m_in, v_in, w_out.T, m_out.T, v_out.T)
    return (loss.reshape(()), *new[:3], *[n.T for n in new[3:]])


def solution(mesh):
    field = P(None, "lat", "lev", None)
    row, first, second = P("lat", None), P("lat", "lev"), P("lev", "lat")
    lats, levs = mesh.shape["lat"], mesh.shape["lev"]

    def body(*arrays):
        step = kernel_body if kernels_fit(arrays, lats, levs) else plain_body
        return step(*arrays)

    return jax.shard_map(
        body,
        mesh=mesh,
        in_specs=(field, field, field, row, row, P(), first, second, first, first, second, second),
        out_specs=(P(), first, first, first, second, second, second),
        check_vma=False,
    )
```

```python
import functools
import math

import jax
import jax.numpy as jnp
from jax import lax
from jax.experimental import pallas as pl
from jax.experimental.pallas import tpu as pltpu
from jax.sharding import PartitionSpec as P

STEP = 7
NOISE_SCALE = 0.5
LEARN_RATE = 0.02
BETA_ONE = 0.9
BETA_TWO = 0.95
EPSILON = 1e-08
WEIGHT_DECAY = 0.1
EVERY = ("lat", "lev")
BF = jnp.bfloat16
F32 = jnp.float32


def adamw(weight, moment_one, moment_two, gradient):
    moment_one = BETA_ONE * moment_one + (1.0 - BETA_ONE) * gradient
    moment_two = BETA_TWO * moment_two + (1.0 - BETA_TWO) * gradient * gradient
    fix_one = 1.0 - BETA_ONE**STEP
    fix_two = 1.0 - BETA_TWO**STEP
    update = moment_one / fix_one / (jnp.sqrt(moment_two / fix_two) + EPSILON)
    return (weight - LEARN_RATE * (update + WEIGHT_DECAY * weight), moment_one, moment_two)


def parts_of(value, count):
    terms = []
    for _ in range(count):
        term = value.astype(BF)
        terms.append(term)
        value = value - lax.optimization_barrier(term).astype(F32)
    return terms


def exchange(pieces, devices):
    flat = jnp.concatenate([p.reshape(devices, -1) for p in pieces], axis=1)
    size = flat.shape[1]
    flat = jnp.pad(flat, ((0, 0), (0, -size % 1024)))
    flat = lax.all_to_all(flat.reshape(devices, -1, 128), EVERY, 0, 0, tiled=True).reshape(devices, -1)
    out, start = [], 0
    for p in pieces:
        count = math.prod(p.shape[1:])
        out.append(lax.slice_in_dim(flat, start, start + count, axis=1).reshape(p.shape))
        start += count
    return out


def plain_body(
    column_state,
    column_target,
    member_noise,
    land_mask,
    legendre_basis,
    mode_filter,
    weight_in,
    weight_out,
    moment_in,
    second_in,
    moment_out,
    second_out,
):
    items, rows, feats, lons = column_state.shape
    members = member_noise.shape[0]
    lats, levs = lax.axis_size("lat"), lax.axis_size("lev")
    devices = lats * levs
    lat_total, all_feats, own = lats * rows, levs * feats, lons // devices
    modes = legendre_basis.shape[1]

    def cut(field):
        field = jnp.moveaxis(field.astype(BF), -1, 0)
        return field.reshape((devices, own) + field.shape[1:])

    def every(value):
        return jnp.broadcast_to(value[None], (devices,) + value.shape)

    def whole(field):
        field = field.reshape(lats, levs, own, -1, rows, feats)
        return field.transpose(3, 0, 4, 2, 1, 5).reshape(-1, lat_total, own, all_feats)

    squares = jnp.sum(member_noise * member_noise, axis=(1, 3))
    mask_count = jnp.sum(land_mask, axis=1).astype(F32)
    got = exchange(
        [
            cut(column_state),
            cut(column_target),
            cut(member_noise),
            cut(land_mask),
            *[every(s) for s in parts_of(squares, 3)],
            every(mask_count.astype(BF)),
            every(legendre_basis.astype(BF)),
            every(weight_in.astype(BF)),
            every(weight_out.astype(BF)),
        ],
        devices,
    )
    state = whole(got[0]).astype(F32)
    target = whole(got[1]).astype(F32)
    noise = whole(got[2]).astype(F32)
    mask = got[3].reshape(lats, levs, own, rows)[:, 0].transpose(0, 2, 1).reshape(lat_total, own).astype(F32)
    squares = sum(g.astype(F32) for g in got[4:7]).reshape(lats, levs, members, feats).sum(0)
    power = squares.transpose(1, 0, 2).reshape(members, all_feats) / (lat_total * lons)
    counts = got[7].reshape(lats, levs, rows)[:, 0].reshape(lat_total).astype(F32)
    basis = got[8].reshape(lats, levs, rows, modes)[:, 0].reshape(lat_total, modes)
    full_in = got[9].reshape(lats, levs, *weight_in.shape).transpose(0, 2, 1, 3).reshape(3 * all_feats, -1)
    full_out = got[10].reshape(lats, levs, *weight_out.shape).transpose(1, 2, 0, 3).reshape(-1, all_feats)

    cosine = jnp.cos((jnp.arange(lat_total, dtype=F32) + 0.5) * (math.pi / lat_total) - 0.5 * math.pi)
    cell_weight = cosine[:, None] * mask
    normaliser = items * all_feats * jnp.sum(cosine * counts)

    scaled = noise * lax.rsqrt(power + 1e-05)[:, None, None, :]
    inputs = (state[:, None] + NOISE_SCALE * scaled[None]).astype(BF)
    padded = jnp.pad(inputs, ((0, 0), (0, 0), (1, 1), (0, 0), (0, 0)))
    stacked = jnp.concatenate([padded[:, :, t : t + lat_total] for t in range(3)], axis=-1)

    def spectral(field):
        coefficients = jnp.einsum("nk,imnlf->imklf", basis, field, preferred_element_type=F32)
        filtered = (mode_filter[:, None, None] * coefficients).astype(BF)
        return jnp.einsum("nk,imklf->imnlf", basis, filtered, preferred_element_type=F32)

    pre_act = jnp.einsum("imnlc,ch->imnlh", stacked, full_in, preferred_element_type=F32)
    hidden = jax.nn.silu(pre_act).astype(BF)
    branch = jnp.einsum("imnlh,hf->imnlf", hidden, full_out, preferred_element_type=F32).astype(BF)
    prediction = state[:, None] + spectral(branch)
    d_one = prediction[:, 0] - target
    d_two = prediction[:, 1] - target
    error_cell = 0.375 * (d_one * d_one + d_two * d_two) + 0.25 * d_one * d_two
    loss_part = jnp.sum(cell_weight[None, :, :, None] * error_cell) / normaliser
    cell_scale = cell_weight[None, :, :, None] / normaliser
    g_one = cell_scale * (0.75 * d_one + 0.25 * d_two)
    g_two = cell_scale * (0.75 * d_two + 0.25 * d_one)
    g_pred = jnp.stack([g_one, g_two], axis=1).astype(BF)
    g_branch = spectral(g_pred).astype(BF)
    g_hidden = jnp.einsum("imnlf,hf->imnlh", g_branch, full_out, preferred_element_type=F32)
    sigmoid = jax.nn.sigmoid(pre_act)
    g_pre = (g_hidden * sigmoid * (1.0 + pre_act * (1.0 - sigmoid))).astype(BF)
    grad_in = jnp.einsum("imnlc,imnlh->ch", stacked, g_pre, preferred_element_type=F32)
    grad_out = jnp.einsum("imnlh,imnlf->hf", hidden, g_branch, preferred_element_type=F32)

    k_in, h_in = weight_in.shape
    h_out, f_out = weight_out.shape
    back = exchange(
        [
            grad_in.astype(BF).reshape(lats, k_in, levs, h_in).transpose(0, 2, 1, 3).reshape(devices, -1),
            grad_out.astype(BF).reshape(levs, h_out, lats, f_out).transpose(2, 0, 1, 3).reshape(devices, -1),
            *[every(t[None]) for t in parts_of(loss_part, 3)],
        ],
        devices,
    )
    grad_in = jnp.sum(back[0].astype(F32), axis=0).reshape(k_in, h_in)
    grad_out = jnp.sum(back[1].astype(F32), axis=0).reshape(h_out, f_out)
    loss_value = sum(jnp.sum(b.astype(F32)) for b in back[2:5])
    new_in = adamw(weight_in, moment_in, second_in, grad_in)
    new_out = adamw(weight_out, moment_out, second_out, grad_out)
    return (loss_value, *new_in, *new_out)


LANES = 128
SUBLANES = 8
NT = (((1,), (1,)), ((), ()))
TN = (((0,), (0,)), ((), ()))
HIGHEST = lax.Precision.HIGHEST


def kernels_fit(arrays, lats, levs):
    items, rows, feats, lons = arrays[0].shape
    members, modes = arrays[2].shape[0], arrays[4].shape[1]
    devices = lats * levs
    return (
        lons == devices * SUBLANES
        and lats * rows * SUBLANES == LANES
        and (rows, feats, levs, members) == (2, LANES // 4, 4, 2)
        and items % 2 == 0
        and lons % LANES == 0
        and modes < LANES
        and arrays[6].shape[0] == 3 * arrays[7].shape[1]
        and arrays[7].shape[1] % 16 == 0
        and arrays[6].shape[1] == arrays[7].shape[0] == LANES // 2
    )


def lane_index(shape):
    return lax.broadcasted_iota(jnp.int32, shape, len(shape) - 1)


def row_index(shape):
    return lax.broadcasted_iota(jnp.int32, shape, len(shape) - 2)


def halves(top, bottom):
    first = lane_index(top.shape) < LANES // 2
    turned_top, turned_bottom = pltpu.roll(top, LANES // 2, 1), pltpu.roll(bottom, LANES // 2, 1)
    return jnp.where(first, top, turned_bottom), jnp.where(first, turned_top, bottom)


def quarters(v):
    a0, a2 = halves(v[0], v[2])
    a1, a3 = halves(v[1], v[3])
    even = lane_index(a0.shape) // 32 % 2 == 0

    def pair(a, b):
        return jnp.where(even, a, pltpu.roll(b, 32, 1)), jnp.where(even, pltpu.roll(a, 96, 1), b)

    return (*pair(a0, a1), *pair(a2, a3))


def pack_kernel(*refs):
    sources, send, arrivals, (aux, arrived) = refs[:8], refs[8], refs[9:17], refs[17:]
    copies = [pltpu.make_async_copy(s, a, arrived.at[n]) for n, (s, a) in enumerate(zip(sources, arrivals))]
    for copy in copies:
        copy.start()
    state, target, noise, mask, basis, mode_filter, first, second = arrivals
    devices, lons = send.shape[0], state.shape[1]
    eye = (row_index((lons, lons)) == lane_index((lons, lons))).astype(BF)

    def turned(rows):
        out = lax.dot_general(eye, rows.astype(BF), NT, preferred_element_type=F32)
        return [out[:, g : g + LANES].reshape(devices, SUBLANES, LANES) for g in range(0, out.shape[1], LANES)]

    for copy in copies:
        copy.wait()
    fields = noise[...]
    groups = turned(state[...]) + turned(target[...]) + turned(fields)
    start = SUBLANES * len(groups)
    send[:, :start, :] = jnp.concatenate(groups, axis=1).astype(BF)

    weights = jnp.concatenate([first[...], second[...]], axis=0)
    quarter = weights.shape[0] // 4
    folded = [
        jnp.concatenate([weights[q * quarter : (q + 1) * quarter, h * 32 : (h + 1) * 32] for q in range(4)], axis=1)
        for h in range(2)
    ]
    folded = jnp.stack(folded).astype(BF)
    pairs = jnp.broadcast_to(folded[None], (devices // 2,) + folded.shape)
    send[:, start : start + quarter, :] = pairs.reshape(devices, quarter, LANES)
    start += quarter

    squares = noise[...] * noise[...]
    upper = squares.astype(BF)
    terms = jnp.concatenate([upper, (squares - upper.astype(F32)).astype(BF)], axis=1)
    total = lax.dot_general(jnp.ones((SUBLANES, 2 * lons), BF), terms, NT, preferred_element_type=F32)
    even = lane_index(total.shape) // 32 % 2 == 0
    total = total + jnp.where(even, pltpu.roll(total, 96, 1), pltpu.roll(total, 32, 1))
    upper = total.astype(BF).astype(F32)
    sums = jnp.where(even, upper, total - upper)[:1]
    cells = mask[...].astype(F32)
    modes = basis.shape[1]
    aux[...] = jnp.zeros_like(aux)
    aux[0:2, 0:modes] = basis[...].astype(BF).astype(F32) * jnp.sqrt(mode_filter[...])
    high = aux[0:2, :].astype(BF).astype(F32)
    low = aux[0:2, :] - high
    counts = jnp.sum(cells, axis=1, keepdims=True)
    high = jnp.where(lane_index(high.shape) == LANES - 1, counts, high)
    spare = jnp.zeros((1, LANES), F32)
    share = LANES // SUBLANES
    for g in range(lons // LANES):
        block = jnp.concatenate([high, low, cells[:, g * LANES : (g + 1) * LANES], sums, spare], axis=0).astype(BF)
        send[g * share : (g + 1) * share, start:, :] = jnp.broadcast_to(block[None], (share, SUBLANES, LANES))


def row_starts(lats, k_in, k_out, quarter):
    return [
        [lat * k_in + q * quarter for q in range(k_in // quarter)]
        + [lats * k_in + lat * k_out + q * quarter for q in range(k_out // quarter)]
        for lat in range(lats)
    ]


def unfold(half, weights, starts):
    lats, levs, quarter, _ = half.shape
    parts = quarters([half[:, lev].astype(F32).reshape(lats * quarter, LANES) for lev in range(levs)])
    for q, part in enumerate(parts):
        for lat in range(lats):
            at = starts[lat][q]
            weights[at : at + quarter, 0:LANES] = part[lat * quarter : (lat + 1) * quarter].astype(BF)


def prepare_kernel(got, stacked, fields, operators, scales, weights, *, items, k_in, k_out, lons, modes):
    lats, levs = got.shape[0], got.shape[1]
    at_aux = got.shape[2] - SUBLANES
    block = (LANES, LANES)
    lat_total = LANES // SUBLANES
    lane, row = lane_index(block), row_index(block)

    quarter = (k_in + k_out) // 4
    own_half = got[:, :, at_aux - quarter : at_aux, :]
    unfold(own_half, weights, row_starts(lats, k_in, k_out, quarter))

    sums = []
    for lev in range(levs):
        total = got[0, lev, at_aux:, :].astype(F32)
        for lat in range(1, lats):
            total = total + got[lat, lev, at_aux:, :].astype(F32)
        sums.append(total)
    sums = [s[6:7] for s in quarters(sums)]
    scale = [lax.rsqrt((sums[2 * m] + sums[2 * m + 1]) / (lat_total * lons) + 1e-05) for m in range(2)]

    def spread(rows):
        return jnp.concatenate([jnp.broadcast_to(r, (SUBLANES, LANES)) for r in rows], axis=0)

    tops = [got[lat, 0, at_aux:, :].astype(F32) for lat in range(lats)]
    high = spread([t[n : n + 1] for t in tops for n in range(2)])
    low = spread([t[n : n + 1] for t in tops for n in range(2, 4)])
    mask_rows = spread([t[n : n + 1] for t in tops for n in range(4, 6)])
    device = lax.axis_index("lat") * levs + lax.axis_index("lev")
    own = lane == device % lat_total * SUBLANES + row % SUBLANES
    mask = jnp.dot(jnp.where(own, mask_rows, 0.0).astype(BF), jnp.ones(block, BF), preferred_element_type=F32)
    latitude = row_index((lat_total, LANES)).astype(F32)
    cosine = jnp.cos((latitude + 0.5) * (math.pi / lat_total) - 0.5 * math.pi)
    cosine = spread([cosine[n : n + 1] for n in range(lat_total)])
    weight_sum = jnp.sum(jnp.where(lane == LANES - 1, cosine * high, 0.0)) / SUBLANES
    scales[...] = cosine * mask / (items * LANES * weight_sum)

    def field_pair(group):
        at = slice(group * SUBLANES, (group + 1) * SUBLANES)
        parts = quarters([got[:, lev, at, :].astype(F32).reshape(lats * SUBLANES, LANES) for lev in range(levs)])
        parts = [q.reshape(lats, 1, SUBLANES, LANES) for q in parts]
        return [jnp.concatenate(parts[2 * k : 2 * k + 2], axis=1).reshape(block) for k in range(2)]

    scaled = [NOISE_SCALE * (f * scale[m]) for m, f in enumerate(field_pair(items))]
    edge = jnp.zeros((SUBLANES, LANES), F32)
    for group in range(items):
        for k, field in enumerate(field_pair(group)):
            fields[2 * group + k] = field.astype(BF)
            if group >= items // 2:
                continue
            for m in range(2):
                x = (field + scaled[m]).astype(BF).astype(F32)
                before = jnp.concatenate([edge, x[:-SUBLANES]], axis=0)
                after = jnp.concatenate([x[SUBLANES:], edge], axis=0)
                at = (2 * (2 * group + k) + m) * LANES
                stacked[at : at + LANES, :] = jnp.concatenate([before, x, after], axis=1).astype(BF)

    root = jnp.where(lane < modes, high + low, 0.0)
    operator = lax.dot_general(root, root, NT, precision=HIGHEST)
    operator = jnp.where(row % SUBLANES == lane % SUBLANES, operator, 0.0)
    high = operator.astype(BF)
    operators[...] = jnp.concatenate([high, (operator - high.astype(F32)).astype(BF)], axis=1)


def step_kernel(
    other, stacked, fields, operators, scales, own, give, keep, losses, weights, hiddens, slopes, g_pres, grads, *, items, k_in, k_out
):
    lats, levs, quarter, _ = other.shape
    taps = lats * k_in
    starts = row_starts(lats, k_in, k_out, quarter)
    unfold(other[...], weights, starts)
    weights[:, LANES:] = own[...]

    operator, cell_scale = operators[...], scales[...]

    def spectral(one, two):
        v = jnp.concatenate([one, two], axis=1)
        out = jnp.dot(operator, jnp.concatenate([v, v], axis=0), preferred_element_type=F32)
        return out[:, :LANES], out[:, LANES:]

    first = weights[0:taps, :]
    second = weights[taps:, :]
    spans = [slice(2 * item * LANES, 2 * (item + 1) * LANES) for item in range(items)]
    branches, gradients, errors = {}, {}, []

    def forward(part):
        rows = stacked.shape[0] // 2
        at = slice(part * rows, (part + 1) * rows)
        pre_act = jnp.dot(stacked[at, :], first, preferred_element_type=F32)
        sigmoid = 0.5 * jnp.tanh(0.5 * pre_act) + 0.5
        hidden = (pre_act * sigmoid).astype(BF)
        hiddens[at, :] = hidden
        slopes[at, :] = sigmoid * (1.0 + pre_act * (1.0 - sigmoid))
        branch = lax.dot_general(hidden, second, NT, preferred_element_type=F32).astype(BF)
        for n in range(items // 2):
            branches[part * (items // 2) + n] = branch[2 * n * LANES : 2 * (n + 1) * LANES]

    def compare(item):
        branch, base, target = branches[item], fields[item].astype(F32), fields[items + item].astype(F32)
        tendency = spectral(branch[:LANES], branch[LANES:])
        d_one = base + tendency[0] - target
        d_two = base + tendency[1] - target
        errors.append(0.375 * (d_one * d_one + d_two * d_two) + 0.25 * d_one * d_two)
        g_one = (cell_scale * (0.75 * d_one + 0.25 * d_two)).astype(BF)
        g_two = (cell_scale * (0.75 * d_two + 0.25 * d_one)).astype(BF)
        gradients[item] = jnp.concatenate(spectral(g_one, g_two), axis=0).astype(BF)

    def backward(part):
        rows = stacked.shape[0] // 2
        at = slice(part * rows, (part + 1) * rows)
        count = items // 2
        g_branch = jnp.concatenate([gradients[n] for n in range(part * count, (part + 1) * count)], axis=0)
        g_hidden = jnp.dot(g_branch, second, preferred_element_type=F32)
        g_pres[at, :] = (g_hidden * slopes[at, :]).astype(BF)

    for part in range(2):
        forward(part)
    for item in range(items):
        compare(item)
    for part in range(2):
        backward(part)
    loss = sum(errors[1:], errors[0])
    grads[0:taps, :] = lax.dot_general(stacked[...], g_pres[...], TN, preferred_element_type=F32)
    g_branch = jnp.concatenate([gradients[item] for item in range(items)], axis=0)
    grads[taps:, :] = lax.dot_general(g_branch, hiddens[...], TN, preferred_element_type=F32)

    loss_part = jnp.sum(loss * cell_scale, keepdims=True)
    terms = []
    for _ in range(3):
        term = loss_part.astype(BF).astype(F32)
        terms.append(jnp.broadcast_to(term, (1, LANES)))
        loss_part = loss_part - term
    terms.append(jnp.zeros((SUBLANES - 3, LANES), F32))
    losses[...] = jnp.concatenate(terms, axis=0).astype(BF)
    for p, half in enumerate((give, keep)):
        columns = slice(p * LANES, (p + 1) * LANES)
        parts = [
            jnp.concatenate([grads[s[q] : s[q] + quarter, columns] for s in starts], axis=0) for q in range(4)
        ]
        for lev, part in enumerate(quarters(parts)):
            half[:, lev] = part.reshape(lats, quarter, LANES).astype(half.dtype)


def join_kernel(keep, came, losses, send):
    quarter = keep.shape[2]
    total = (keep[...] + came[...].astype(F32)).astype(BF)
    send[:, :quarter, :] = total.reshape(-1, quarter, LANES)
    send[:, quarter:, :] = jnp.broadcast_to(losses[...][None], (send.shape[0], SUBLANES, LANES))


def update_kernel(got, w_in, m_in, v_in, w_out, m_out, v_out, loss, nw_in, nm_in, nv_in, nw_out, nm_out, nv_out):
    total = jnp.sum(got[...].astype(F32), axis=0)
    at_loss = total.shape[1] - SUBLANES

    def unfolded(rows):
        return jnp.concatenate([rows[:, q * 32 : (q + 1) * 32] for q in range(4)], axis=0)

    gradient = jnp.concatenate([unfolded(total[h, :at_loss]) for h in range(2)], axis=1)
    k_in = w_in.shape[0]
    nw_in[...], nm_in[...], nv_in[...] = adamw(w_in[...], m_in[...], v_in[...], gradient[:k_in])
    nw_out[...], nm_out[...], nv_out[...] = adamw(w_out[...], m_out[...], v_out[...], gradient[k_in:])
    loss[...] = jnp.sum(total[0, at_loss:, :1] + total[1, at_loss:, :1], axis=0, keepdims=True)


def kernel_body(state, target, noise, mask, basis, mode_filter, w_in, w_out, m_in, v_in, m_out, v_out):
    items, _, _, lons = state.shape
    lats, levs = lax.axis_size("lat"), lax.axis_size("lev")
    devices = lats * levs
    k_in, k_out, modes = w_in.shape[0], w_out.shape[1], basis.shape[1]
    quarter = (k_in + k_out) // 4
    at_weights = SUBLANES * (items + 1)
    rows = at_weights + quarter + SUBLANES
    inputs, cells = lats * (k_in + k_out), 2 * items * LANES
    partners = [(i, i ^ 1) for i in range(levs)]
    vmem, hbm = pl.BlockSpec(memory_space=pltpu.VMEM), pl.BlockSpec(memory_space=pltpu.HBM)
    small = pltpu.CompilerParams(vmem_limit_bytes=8 * 2**20)

    def shape(*dims, kind=F32):
        return jax.ShapeDtypeStruct(dims, kind)

    sources = (
        state.reshape(-1, lons),
        target.reshape(-1, lons),
        noise.reshape(-1, lons),
        mask,
        basis,
        mode_filter[None],
        w_in,
        w_out.T,
    )
    send = pl.pallas_call(
        pack_kernel,
        out_shape=shape(devices, rows, LANES, kind=BF),
        in_specs=[hbm] * len(sources),
        scratch_shapes=[
            *[pltpu.VMEM(s.shape, s.dtype) for s in sources],
            pltpu.VMEM((SUBLANES, LANES), F32),
            pltpu.SemaphoreType.DMA((len(sources),)),
        ],
        name="pack",
    )(*sources)
    got = lax.all_to_all(send, EVERY, 0, 0, tiled=True).reshape(lats, levs, rows, LANES)
    own = got[:, :, at_weights : at_weights + quarter]
    other = lax.ppermute(own, "lev", partners)
    prepared = pl.pallas_call(
        functools.partial(prepare_kernel, items=items, k_in=k_in, k_out=k_out, lons=lons, modes=modes),
        out_shape=(
            shape(cells, 3 * LANES, kind=BF),
            shape(2 * items, LANES, LANES, kind=BF),
            shape(LANES, 2 * LANES, kind=BF),
            shape(LANES, LANES),
            shape(inputs, LANES, kind=BF),
        ),
        in_specs=[vmem],
        compiler_params=small,
        cost_estimate=pl.CostEstimate(flops=2**22, bytes_accessed=2**22, transcendentals=0),
        name="prepare",
    )(got)
    block = (lats, levs, quarter, LANES)
    give, keep, losses = pl.pallas_call(
        functools.partial(step_kernel, items=items, k_in=k_in, k_out=k_out),
        out_shape=(shape(*block, kind=BF), shape(*block), shape(SUBLANES, LANES, kind=BF)),
        scratch_shapes=[
            pltpu.VMEM((inputs, 2 * LANES), BF),
            pltpu.VMEM((cells, 2 * LANES), BF),
            pltpu.VMEM((cells, 2 * LANES), F32),
            pltpu.VMEM((cells, 2 * LANES), BF),
            pltpu.VMEM((inputs, 2 * LANES), F32),
        ],
        compiler_params=pltpu.CompilerParams(vmem_limit_bytes=16 * 2**20),
        name="step",
    )(other, *prepared)
    came = lax.ppermute(give, "lev", partners)
    back = pl.pallas_call(
        join_kernel,
        out_shape=shape(devices, quarter + SUBLANES, LANES, kind=BF),
        compiler_params=small,
        name="join",
    )(keep, came, losses)
    back = lax.all_to_all(back, EVERY, 0, 0, tiled=True)
    wide, tall = shape(*w_in.shape), shape(*w_out.shape[::-1])
    loss, *new = pl.pallas_call(
        update_kernel,
        out_shape=(shape(1, 1), wide, wide, wide, tall, tall, tall),
        compiler_params=small,
        name="update",
    )(back.reshape(-1, 2, quarter + SUBLANES, LANES), w_in, m_in, v_in, w_out.T, m_out.T, v_out.T)
    return (loss.reshape(()), *new[:3], *[n.T for n in new[3:]])


def solution(mesh):
    field = P(None, "lat", "lev", None)
    row, first, second = P("lat", None), P("lat", "lev"), P("lev", "lat")
    lats, levs = mesh.shape["lat"], mesh.shape["lev"]

    def body(*arrays):
        step = kernel_body if kernels_fit(arrays, lats, levs) else plain_body
        return step(*arrays)

    return jax.shard_map(
        body,
        mesh=mesh,
        in_specs=(field, field, field, row, row, P(), first, second, first, first, second, second),
        out_specs=(P(), first, first, first, second, second, second),
        check_vma=False,
    )
```

```python
import functools
import math

import jax
import jax.numpy as jnp
from jax import lax
from jax.experimental import pallas as pl
from jax.experimental.pallas import tpu as pltpu
from jax.sharding import PartitionSpec as P

STEP = 7
NOISE_SCALE = 0.5
LEARN_RATE = 0.02
BETA_ONE = 0.9
BETA_TWO = 0.95
EPSILON = 1e-08
WEIGHT_DECAY = 0.1
LAT, LEV = ("far", "near"), ("side", "core")
EVERY = LAT + LEV
BF = jnp.bfloat16
F32 = jnp.float32


def adamw(weight, moment_one, moment_two, gradient):
    moment_one = BETA_ONE * moment_one + (1.0 - BETA_ONE) * gradient
    moment_two = BETA_TWO * moment_two + (1.0 - BETA_TWO) * gradient * gradient
    fix_one = 1.0 - BETA_ONE**STEP
    fix_two = 1.0 - BETA_TWO**STEP
    update = moment_one / fix_one / (jnp.sqrt(moment_two / fix_two) + EPSILON)
    return (weight - LEARN_RATE * (update + WEIGHT_DECAY * weight), moment_one, moment_two)


def parts_of(value, count):
    terms = []
    for _ in range(count):
        term = value.astype(BF)
        terms.append(term)
        value = value - lax.optimization_barrier(term).astype(F32)
    return terms


def exchange(pieces, devices):
    flat = jnp.concatenate([p.reshape(devices, -1) for p in pieces], axis=1)
    size = flat.shape[1]
    flat = jnp.pad(flat, ((0, 0), (0, -size % 1024)))
    flat = lax.all_to_all(flat.reshape(devices, -1, 128), EVERY, 0, 0, tiled=True).reshape(devices, -1)
    out, start = [], 0
    for p in pieces:
        count = math.prod(p.shape[1:])
        out.append(lax.slice_in_dim(flat, start, start + count, axis=1).reshape(p.shape))
        start += count
    return out


def plain_body(
    column_state,
    column_target,
    member_noise,
    land_mask,
    legendre_basis,
    mode_filter,
    weight_in,
    weight_out,
    moment_in,
    second_in,
    moment_out,
    second_out,
):
    items, rows, feats, lons = column_state.shape
    members = member_noise.shape[0]
    lats, levs = lax.axis_size(LAT), lax.axis_size(LEV)
    devices = lats * levs
    lat_total, all_feats, own = lats * rows, levs * feats, lons // devices
    modes = legendre_basis.shape[1]

    def cut(field):
        field = jnp.moveaxis(field.astype(BF), -1, 0)
        return field.reshape((devices, own) + field.shape[1:])

    def every(value):
        return jnp.broadcast_to(value[None], (devices,) + value.shape)

    def whole(field):
        field = field.reshape(lats, levs, own, -1, rows, feats)
        return field.transpose(3, 0, 4, 2, 1, 5).reshape(-1, lat_total, own, all_feats)

    squares = jnp.sum(member_noise * member_noise, axis=(1, 3))
    mask_count = jnp.sum(land_mask, axis=1).astype(F32)
    got = exchange(
        [
            cut(column_state),
            cut(column_target),
            cut(member_noise),
            cut(land_mask),
            *[every(s) for s in parts_of(squares, 3)],
            every(mask_count.astype(BF)),
            every(legendre_basis.astype(BF)),
            every(weight_in.astype(BF)),
            every(weight_out.astype(BF)),
        ],
        devices,
    )
    state = whole(got[0]).astype(F32)
    target = whole(got[1]).astype(F32)
    noise = whole(got[2]).astype(F32)
    mask = got[3].reshape(lats, levs, own, rows)[:, 0].transpose(0, 2, 1).reshape(lat_total, own).astype(F32)
    squares = sum(g.astype(F32) for g in got[4:7]).reshape(lats, levs, members, feats).sum(0)
    power = squares.transpose(1, 0, 2).reshape(members, all_feats) / (lat_total * lons)
    counts = got[7].reshape(lats, levs, rows)[:, 0].reshape(lat_total).astype(F32)
    basis = got[8].reshape(lats, levs, rows, modes)[:, 0].reshape(lat_total, modes)
    full_in = got[9].reshape(lats, levs, *weight_in.shape).transpose(0, 2, 1, 3).reshape(3 * all_feats, -1)
    full_out = got[10].reshape(lats, levs, *weight_out.shape).transpose(1, 2, 0, 3).reshape(-1, all_feats)

    cosine = jnp.cos((jnp.arange(lat_total, dtype=F32) + 0.5) * (math.pi / lat_total) - 0.5 * math.pi)
    cell_weight = cosine[:, None] * mask
    normaliser = items * all_feats * jnp.sum(cosine * counts)

    scaled = noise * lax.rsqrt(power + 1e-05)[:, None, None, :]
    inputs = (state[:, None] + NOISE_SCALE * scaled[None]).astype(BF)
    padded = jnp.pad(inputs, ((0, 0), (0, 0), (1, 1), (0, 0), (0, 0)))
    stacked = jnp.concatenate([padded[:, :, t : t + lat_total] for t in range(3)], axis=-1)

    def spectral(field):
        coefficients = jnp.einsum("nk,imnlf->imklf", basis, field, preferred_element_type=F32)
        filtered = (mode_filter[:, None, None] * coefficients).astype(BF)
        return jnp.einsum("nk,imklf->imnlf", basis, filtered, preferred_element_type=F32)

    pre_act = jnp.einsum("imnlc,ch->imnlh", stacked, full_in, preferred_element_type=F32)
    hidden = jax.nn.silu(pre_act).astype(BF)
    branch = jnp.einsum("imnlh,hf->imnlf", hidden, full_out, preferred_element_type=F32).astype(BF)
    prediction = state[:, None] + spectral(branch)
    d_one = prediction[:, 0] - target
    d_two = prediction[:, 1] - target
    error_cell = 0.375 * (d_one * d_one + d_two * d_two) + 0.25 * d_one * d_two
    loss_part = jnp.sum(cell_weight[None, :, :, None] * error_cell) / normaliser
    cell_scale = cell_weight[None, :, :, None] / normaliser
    g_one = cell_scale * (0.75 * d_one + 0.25 * d_two)
    g_two = cell_scale * (0.75 * d_two + 0.25 * d_one)
    g_pred = jnp.stack([g_one, g_two], axis=1).astype(BF)
    g_branch = spectral(g_pred).astype(BF)
    g_hidden = jnp.einsum("imnlf,hf->imnlh", g_branch, full_out, preferred_element_type=F32)
    sigmoid = jax.nn.sigmoid(pre_act)
    g_pre = (g_hidden * sigmoid * (1.0 + pre_act * (1.0 - sigmoid))).astype(BF)
    grad_in = jnp.einsum("imnlc,imnlh->ch", stacked, g_pre, preferred_element_type=F32)
    grad_out = jnp.einsum("imnlh,imnlf->hf", hidden, g_branch, preferred_element_type=F32)

    k_in, h_in = weight_in.shape
    h_out, f_out = weight_out.shape
    back = exchange(
        [
            grad_in.astype(BF).reshape(lats, k_in, levs, h_in).transpose(0, 2, 1, 3).reshape(devices, -1),
            grad_out.astype(BF).reshape(levs, h_out, lats, f_out).transpose(2, 0, 1, 3).reshape(devices, -1),
            *[every(t[None]) for t in parts_of(loss_part, 3)],
        ],
        devices,
    )
    grad_in = jnp.sum(back[0].astype(F32), axis=0).reshape(k_in, h_in)
    grad_out = jnp.sum(back[1].astype(F32), axis=0).reshape(h_out, f_out)
    loss_value = sum(jnp.sum(b.astype(F32)) for b in back[2:5])
    new_in = adamw(weight_in, moment_in, second_in, grad_in)
    new_out = adamw(weight_out, moment_out, second_out, grad_out)
    return (loss_value, *new_in, *new_out)


LANES = 128
SUBLANES = 8
NT = (((1,), (1,)), ((), ()))
TN = (((0,), (0,)), ((), ()))
HIGHEST = lax.Precision.HIGHEST


def kernels_fit(arrays, lats, levs):
    items, rows, feats, lons = arrays[0].shape
    members, modes = arrays[2].shape[0], arrays[4].shape[1]
    devices = lats * levs
    return (
        lons == devices * SUBLANES
        and lats * rows * SUBLANES == LANES
        and (rows, feats, levs, members) == (2, LANES // 4, 4, 2)
        and items % 2 == 0
        and lons % LANES == 0
        and modes < LANES
        and arrays[6].shape[0] == 3 * arrays[7].shape[1]
        and arrays[7].shape[1] % 16 == 0
        and arrays[6].shape[1] == arrays[7].shape[0] == LANES // 2
    )


def lane_index(shape):
    return lax.broadcasted_iota(jnp.int32, shape, len(shape) - 1)


def row_index(shape):
    return lax.broadcasted_iota(jnp.int32, shape, len(shape) - 2)


def halves(top, bottom):
    first = lane_index(top.shape) < LANES // 2
    turned_top, turned_bottom = pltpu.roll(top, LANES // 2, 1), pltpu.roll(bottom, LANES // 2, 1)
    return jnp.where(first, top, turned_bottom), jnp.where(first, turned_top, bottom)


def quarters(v):
    a0, a2 = halves(v[0], v[2])
    a1, a3 = halves(v[1], v[3])
    even = lane_index(a0.shape) // 32 % 2 == 0

    def pair(a, b):
        return jnp.where(even, a, pltpu.roll(b, 32, 1)), jnp.where(even, pltpu.roll(a, 96, 1), b)

    return (*pair(a0, a1), *pair(a2, a3))


def pack_kernel(*refs):
    sources, send, arrivals, (aux, arrived) = refs[:8], refs[8], refs[9:17], refs[17:]
    copies = [pltpu.make_async_copy(s, a, arrived.at[n]) for n, (s, a) in enumerate(zip(sources, arrivals))]
    for copy in copies:
        copy.start()
    state, target, noise, mask, basis, mode_filter, first, second = arrivals
    devices, lons = send.shape[0], state.shape[1]
    eye = (row_index((lons, lons)) == lane_index((lons, lons))).astype(BF)

    def turned(rows):
        out = lax.dot_general(eye, rows.astype(BF), NT, preferred_element_type=F32)
        return [out[:, g : g + LANES].reshape(devices, SUBLANES, LANES) for g in range(0, out.shape[1], LANES)]

    for copy in copies:
        copy.wait()
    fields = noise[...]
    groups = turned(state[...]) + turned(target[...]) + turned(fields)
    start = SUBLANES * len(groups)
    send[:, :start, :] = jnp.concatenate(groups, axis=1).astype(BF)

    weights = jnp.concatenate([first[...], second[...]], axis=0)
    quarter = weights.shape[0] // 4
    folded = [
        jnp.concatenate([weights[q * quarter : (q + 1) * quarter, h * 32 : (h + 1) * 32] for q in range(4)], axis=1)
        for h in range(2)
    ]
    folded = jnp.stack(folded).astype(BF)
    pairs = jnp.broadcast_to(folded[None, :, None], (2, 2, devices // 4) + folded.shape[1:])
    send[:, start : start + quarter, :] = pairs.reshape(devices, quarter, LANES)
    start += quarter

    squares = noise[...] * noise[...]
    upper = squares.astype(BF)
    terms = jnp.concatenate([upper, (squares - upper.astype(F32)).astype(BF)], axis=1)
    total = lax.dot_general(jnp.ones((SUBLANES, 2 * lons), BF), terms, NT, preferred_element_type=F32)
    even = lane_index(total.shape) // 32 % 2 == 0
    total = total + jnp.where(even, pltpu.roll(total, 96, 1), pltpu.roll(total, 32, 1))
    upper = total.astype(BF).astype(F32)
    sums = jnp.where(even, upper, total - upper)[:1]
    cells = mask[...].astype(F32)
    modes = basis.shape[1]
    aux[...] = jnp.zeros_like(aux)
    aux[0:2, 0:modes] = basis[...].astype(BF).astype(F32) * jnp.sqrt(mode_filter[...])
    high = aux[0:2, :].astype(BF).astype(F32)
    low = aux[0:2, :] - high
    counts = jnp.sum(cells, axis=1, keepdims=True)
    high = jnp.where(lane_index(high.shape) == LANES - 1, counts, high)
    spare = jnp.zeros((1, LANES), F32)
    share = LANES // SUBLANES
    for g in range(lons // LANES):
        block = jnp.concatenate([high, low, cells[:, g * LANES : (g + 1) * LANES], sums, spare], axis=0).astype(BF)
        send[g * share : (g + 1) * share, start:, :] = jnp.broadcast_to(block[None], (share, SUBLANES, LANES))


def place(lat, lev, far):
    return ((lat % 2 * 2 + lev % 2) * 2 + lev // 2) * far + lat // 2


def back_place(lat, lev, far):
    return ((lat % 2 * 2 + lev % 2) * far + lat // 2) * 2 + lev // 2


def of_lev(got, lev, at):
    lats = got.shape[0] // 4
    return jnp.concatenate([got[place(lat, lev, lats // 2), at, :].astype(F32) for lat in range(lats)], axis=0)


def row_starts(lats, k_in, k_out, quarter):
    return [
        [lat * k_in + q * quarter for q in range(k_in // quarter)]
        + [lats * k_in + lat * k_out + q * quarter for q in range(k_out // quarter)]
        for lat in range(lats)
    ]


def unfold(half, at, weights, starts):
    quarter = at.stop - at.start
    for q, part in enumerate(quarters([of_lev(half, lev, at) for lev in range(4)])):
        for lat in range(len(starts)):
            at = starts[lat][q]
            weights[at : at + quarter, 0:LANES] = part[lat * quarter : (lat + 1) * quarter].astype(BF)


def forward(stacked, weights, taps, at, hiddens, slopes, branches):
    pre_act = jnp.dot(stacked[at, :], weights[0:taps, :], preferred_element_type=F32)
    sigmoid = 0.5 * jnp.tanh(0.5 * pre_act) + 0.5
    hidden = (pre_act * sigmoid).astype(BF)
    hiddens[at, :] = hidden
    slopes[at, :] = sigmoid * (1.0 + pre_act * (1.0 - sigmoid))
    share = lax.dot_general(hidden, weights[taps:, :], NT, preferred_element_type=F32)
    if branches is None:
        return share
    branches[at, :] = share


def fold_gradients(stacked, g_pres, g_branch, hiddens, taps, starts, quarter, grads, out):
    lats, levs = out.shape[0], out.shape[1]
    grads[0:taps, :] = lax.dot_general(stacked, g_pres, TN, preferred_element_type=F32)
    grads[taps:, :] = lax.dot_general(g_branch, hiddens, TN, preferred_element_type=F32)
    parts = [jnp.concatenate([grads[s[q] : s[q] + quarter, :] for s in starts], axis=0) for q in range(4)]
    for lev, part in enumerate(quarters(parts)):
        out[:, lev] = part.reshape(lats, quarter, LANES).astype(out.dtype)


def prepare_kernel(got, stacked, fields, operators, scales, weights, hiddens, slopes, branches, *, items, k_in, k_out, lons, modes):
    lats, levs = got.shape[0] // 4, 4
    at_aux = got.shape[1] - SUBLANES
    block = (LANES, LANES)
    lat_total = LANES // SUBLANES
    lane, row = lane_index(block), row_index(block)

    quarter = (k_in + k_out) // 4
    unfold(got, slice(at_aux - quarter, at_aux), weights, row_starts(lats, k_in, k_out, quarter))

    sums = []
    for lev in range(levs):
        total = of_lev(got, lev, slice(at_aux, at_aux + SUBLANES))
        sums.append(jnp.sum(total.reshape(lats, SUBLANES, LANES), axis=0))
    sums = [s[6:7] for s in quarters(sums)]
    scale = [lax.rsqrt((sums[2 * m] + sums[2 * m + 1]) / (lat_total * lons) + 1e-05) for m in range(2)]

    def spread(rows):
        return jnp.concatenate([jnp.broadcast_to(r, (SUBLANES, LANES)) for r in rows], axis=0)

    tops = [got[place(lat, 0, lats // 2), at_aux:, :].astype(F32) for lat in range(lats)]
    high = spread([t[n : n + 1] for t in tops for n in range(2)])
    low = spread([t[n : n + 1] for t in tops for n in range(2, 4)])
    mask_rows = spread([t[n : n + 1] for t in tops for n in range(4, 6)])
    lat = lax.axis_index("far") * 2 + lax.axis_index("near")
    device = place(lat, lax.axis_index("side") * 2 + lax.axis_index("core"), lats // 2)
    own = lane == device % lat_total * SUBLANES + row % SUBLANES
    mask = jnp.dot(jnp.where(own, mask_rows, 0.0).astype(BF), jnp.ones(block, BF), preferred_element_type=F32)
    latitude = row_index((lat_total, LANES)).astype(F32)
    cosine = jnp.cos((latitude + 0.5) * (math.pi / lat_total) - 0.5 * math.pi)
    cosine = spread([cosine[n : n + 1] for n in range(lat_total)])
    weight_sum = jnp.sum(jnp.where(lane == LANES - 1, cosine * high, 0.0)) / SUBLANES
    scales[...] = cosine * mask / (items * LANES * weight_sum)

    def field_pair(group):
        at = slice(group * SUBLANES, (group + 1) * SUBLANES)
        parts = quarters([of_lev(got, lev, at) for lev in range(levs)])
        parts = [q.reshape(lats, 1, SUBLANES, LANES) for q in parts]
        return [jnp.concatenate(parts[2 * k : 2 * k + 2], axis=1).reshape(block) for k in range(2)]

    scaled = [NOISE_SCALE * (f * scale[m]) for m, f in enumerate(field_pair(items))]
    edge = jnp.zeros((SUBLANES, LANES), F32)
    for group in range(items):
        for k, field in enumerate(field_pair(group)):
            fields[2 * group + k] = field.astype(BF)
            if group >= items // 2:
                continue
            for m in range(2):
                x = (field + scaled[m]).astype(BF).astype(F32)
                before = jnp.concatenate([edge, x[:-SUBLANES]], axis=0)
                after = jnp.concatenate([x[SUBLANES:], edge], axis=0)
                at = (2 * (2 * group + k) + m) * LANES
                stacked[at : at + LANES, :] = jnp.concatenate([before, x, after], axis=1).astype(BF)

    root = jnp.where(lane < modes, high + low, 0.0)
    operator = lax.dot_general(root, root, NT, precision=HIGHEST)
    operator = jnp.where(row % SUBLANES == lane % SUBLANES, operator, 0.0)
    high = operator.astype(BF)
    operators[...] = jnp.concatenate([high, (operator - high.astype(F32)).astype(BF)], axis=1)

    taps = lats * k_in
    for part in range(2):
        at = slice(part * items * LANES, (part + 1) * items * LANES)
        forward(stacked, weights, taps, at, hiddens, slopes, branches)


def step_kernel(
    other, stacked, fields, operators, scales, own_branches, give, losses, g_branches, weights, hiddens, slopes, g_pres, grads,
    *, items, k_in, k_out
):
    lats, quarter = other.shape[0] // 4, other.shape[1]
    taps = lats * k_in
    starts = row_starts(lats, k_in, k_out, quarter)
    unfold(other, slice(0, quarter), weights, starts)
    operator, cell_scale = operators[...], scales[...]

    def spectral(one, two):
        v = jnp.concatenate([one, two], axis=1)
        out = jnp.dot(operator, jnp.concatenate([v, v], axis=0), preferred_element_type=F32)
        return out[:, :LANES], out[:, LANES:]

    branches, gradients, errors = {}, {}, []
    halves_of_items = [range(part * items // 2, (part + 1) * items // 2) for part in range(2)]

    def cells_of(chosen):
        return slice(2 * chosen[0] * LANES, 2 * (chosen[-1] + 1) * LANES)

    for chosen in halves_of_items:
        at = cells_of(chosen)
        branch = (own_branches[at, :] + forward(stacked, weights, taps, at, hiddens, slopes, None)).astype(BF)
        for place, item in enumerate(chosen):
            branches[item] = branch[2 * place * LANES : 2 * (place + 1) * LANES]

    for item in range(items):
        branch, base, target = branches[item], fields[item].astype(F32), fields[items + item].astype(F32)
        tendency = spectral(branch[:LANES], branch[LANES:])
        d_one = base + tendency[0] - target
        d_two = base + tendency[1] - target
        errors.append(0.375 * (d_one * d_one + d_two * d_two) + 0.25 * d_one * d_two)
        g_one = (cell_scale * (0.75 * d_one + 0.25 * d_two)).astype(BF)
        g_two = (cell_scale * (0.75 * d_two + 0.25 * d_one)).astype(BF)
        gradients[item] = jnp.concatenate(spectral(g_one, g_two), axis=0).astype(BF)

    for chosen in halves_of_items:
        at = cells_of(chosen)
        g_branch = jnp.concatenate([gradients[item] for item in chosen], axis=0)
        g_branches[at, :] = g_branch
        g_hidden = jnp.dot(g_branch, weights[taps:, :], preferred_element_type=F32)
        g_pres[at, :] = (g_hidden * slopes[at, :]).astype(BF)
    fold_gradients(stacked[...], g_pres[...], g_branches[...], hiddens[...], taps, starts, quarter, grads, give)

    loss = sum(errors[1:], errors[0])
    loss_part = jnp.sum(loss * cell_scale, keepdims=True)
    terms = []
    for _ in range(3):
        term = loss_part.astype(BF).astype(F32)
        terms.append(jnp.broadcast_to(term, (1, LANES)))
        loss_part = loss_part - term
    terms.append(jnp.zeros((SUBLANES - 3, LANES), F32))
    losses[...] = jnp.concatenate(terms, axis=0).astype(BF)


def keep_kernel(stacked, own, hiddens, slopes, g_branches, keep, g_pres, grads, *, k_in, k_out):
    lats, quarter = keep.shape[0], keep.shape[2]
    taps, cells = lats * k_in, stacked.shape[0]
    for part in range(2):
        at = slice(part * cells // 2, (part + 1) * cells // 2)
        g_hidden = jnp.dot(g_branches[at, :], own[taps:, :], preferred_element_type=F32)
        g_pres[at, :] = (g_hidden * slopes[at, :]).astype(BF)
    starts = row_starts(lats, k_in, k_out, quarter)
    fold_gradients(stacked[...], g_pres[...], g_branches[...], hiddens[...], taps, starts, quarter, grads, keep)


def join_kernel(keep, came, losses, send):
    lats, levs, quarter, _ = keep.shape
    total = (keep[...] + came[...].astype(F32)).astype(BF)
    for lat in range(lats):
        for lev in range(levs):
            send[back_place(lat, lev, lats // 2), :quarter, :] = total[lat, lev]
    send[:, quarter:, :] = jnp.broadcast_to(losses[...][None], (send.shape[0], SUBLANES, LANES))


def update_kernel(got, w_in, m_in, v_in, w_out, m_out, v_out, loss, nw_in, nm_in, nv_in, nw_out, nm_out, nv_out):
    total = jnp.sum(jnp.sum(got[...].astype(F32), axis=2), axis=0)
    at_loss = total.shape[1] - SUBLANES

    def unfolded(rows):
        return jnp.concatenate([rows[:, q * 32 : (q + 1) * 32] for q in range(4)], axis=0)

    gradient = jnp.concatenate([unfolded(total[h, :at_loss]) for h in range(2)], axis=1)
    k_in = w_in.shape[0]
    nw_in[...], nm_in[...], nv_in[...] = adamw(w_in[...], m_in[...], v_in[...], gradient[:k_in])
    nw_out[...], nm_out[...], nv_out[...] = adamw(w_out[...], m_out[...], v_out[...], gradient[k_in:])
    loss[...] = jnp.sum(total[0, at_loss:, :1] + total[1, at_loss:, :1], axis=0, keepdims=True)


def kernel_body(state, target, noise, mask, basis, mode_filter, w_in, w_out, m_in, v_in, m_out, v_out):
    items, _, _, lons = state.shape
    far, levs = lax.axis_size("far"), 4
    lats, devices = 2 * far, 8 * far
    k_in, k_out, modes = w_in.shape[0], w_out.shape[1], basis.shape[1]
    quarter = (k_in + k_out) // 4
    at_weights = SUBLANES * (items + 1)
    rows = at_weights + quarter + SUBLANES
    inputs, cells = lats * (k_in + k_out), 2 * items * LANES
    partners = [(0, 1), (1, 0)]
    vmem, hbm = pl.BlockSpec(memory_space=pltpu.VMEM), pl.BlockSpec(memory_space=pltpu.HBM)
    small = pltpu.CompilerParams(vmem_limit_bytes=8 * 2**20)

    def shape(*dims, kind=F32):
        return jax.ShapeDtypeStruct(dims, kind)

    sources = (
        state.reshape(-1, lons),
        target.reshape(-1, lons),
        noise.reshape(-1, lons),
        mask,
        basis,
        mode_filter[None],
        w_in,
        w_out.T,
    )
    send = pl.pallas_call(
        pack_kernel,
        out_shape=shape(devices, rows, LANES, kind=BF),
        in_specs=[hbm] * len(sources),
        scratch_shapes=[
            *[pltpu.VMEM(s.shape, s.dtype) for s in sources],
            pltpu.VMEM((SUBLANES, LANES), F32),
            pltpu.SemaphoreType.DMA((len(sources),)),
        ],
        name="pack",
    )(*sources)
    got = lax.all_to_all(send, ("near", "core", "side", "far"), 0, 0, tiled=True)
    other = lax.ppermute(got[:, at_weights : at_weights + quarter], "core", partners)
    stacked, fields, operators, scales, own, hiddens, slopes, branches = pl.pallas_call(
        functools.partial(prepare_kernel, items=items, k_in=k_in, k_out=k_out, lons=lons, modes=modes),
        out_shape=(
            shape(cells, 3 * LANES, kind=BF),
            shape(2 * items, LANES, LANES, kind=BF),
            shape(LANES, 2 * LANES, kind=BF),
            shape(LANES, LANES),
            shape(inputs, LANES, kind=BF),
            shape(cells, LANES, kind=BF),
            shape(cells, LANES),
            shape(cells, LANES),
        ),
        in_specs=[vmem],
        compiler_params=small,
        cost_estimate=pl.CostEstimate(flops=2**28, bytes_accessed=2**22, transcendentals=0),
        name="prepare",
    )(got)
    block = (lats, levs, quarter, LANES)
    give, losses, g_branches = pl.pallas_call(
        functools.partial(step_kernel, items=items, k_in=k_in, k_out=k_out),
        out_shape=(shape(*block, kind=BF), shape(SUBLANES, LANES, kind=BF), shape(cells, LANES, kind=BF)),
        scratch_shapes=[
            pltpu.VMEM((inputs, LANES), BF),
            pltpu.VMEM((cells, LANES), BF),
            pltpu.VMEM((cells, LANES), F32),
            pltpu.VMEM((cells, LANES), BF),
            pltpu.VMEM((inputs, LANES), F32),
        ],
        compiler_params=pltpu.CompilerParams(vmem_limit_bytes=16 * 2**20),
        name="step",
    )(other, stacked, fields, operators, scales, branches)
    came = lax.ppermute(give, "core", partners)
    keep = pl.pallas_call(
        functools.partial(keep_kernel, k_in=k_in, k_out=k_out),
        out_shape=shape(*block),
        scratch_shapes=[pltpu.VMEM((cells, LANES), BF), pltpu.VMEM((inputs, LANES), F32)],
        compiler_params=small,
        cost_estimate=pl.CostEstimate(flops=2**28, bytes_accessed=2**22, transcendentals=0),
        name="keep",
    )(stacked, own, hiddens, slopes, g_branches)
    back = pl.pallas_call(
        join_kernel,
        out_shape=shape(devices, quarter + SUBLANES, LANES, kind=BF),
        compiler_params=small,
        name="join",
    )(keep, came, losses)
    back = lax.all_to_all(back, ("near", "core", "far", "side"), 0, 0, tiled=True)
    wide, tall = shape(*w_in.shape), shape(*w_out.shape[::-1])
    loss, *new = pl.pallas_call(
        update_kernel,
        out_shape=(shape(1, 1), wide, wide, wide, tall, tall, tall),
        compiler_params=small,
        name="update",
    )(back.reshape(2, 2, devices // 4, quarter + SUBLANES, LANES), w_in, m_in, v_in, w_out.T, m_out.T, v_out.T)
    return (loss.reshape(()), *new[:3], *[n.T for n in new[3:]])


def solution(mesh):
    lats, levs = mesh.shape["lat"], mesh.shape["lev"]
    near, core = math.gcd(lats, 2), math.gcd(levs, 2)
    finer = jax.sharding.Mesh(mesh.devices.reshape(lats // near, near, levs // core, core), EVERY)
    field = P(None, LAT, LEV, None)
    row, first, second = P(LAT, None), P(LAT, LEV), P(LEV, LAT)

    def body(*arrays):
        step = kernel_body if kernels_fit(arrays, lats, levs) else plain_body
        return step(*arrays)

    return jax.shard_map(
        body,
        mesh=finer,
        in_specs=(field, field, field, row, row, P(), first, second, first, first, second, second),
        out_specs=(P(), first, first, first, second, second, second),
        check_vma=False,
    )
```
